32 devices in a mesh: groups: 2 (over x), shard: 16 (over z, y, core).
Axes of the slice: x: 2, y: 2, z: 4, core: 2. Of those that a mesh axis runs over, the one named last changes fastest.
Arguments:
- kv_store: bfloat16 [64, 256, 2048], P(('groups', 'shard')), parts along dimension 0, may hold values from -6 to 6
- block_order: int32 [64], P(('groups', 'shard')), parts along dimension 0, may hold values from 0 to 31, as said below
- lengths: int32 [16], P('groups'), parts along dimension 0, may hold values from 1 to 12, as said below
- row_positions: int32 [16, 128], P('groups'), parts along dimension 0, may hold values from 0 to 3071, as said below
- queries: bfloat16 [256, 65536], P('groups', 'shard'), parts along dimension 0, may hold values from -48 to 48
- fresh_rows: bfloat16 [256, 16384], P('groups', 'shard'), parts along dimension 0, may hold values from -280 to 280
Outputs:
- attended: bfloat16 [256, 65536], P('groups', 'shard'), parts along dimension 0
The draws below stay inside these ranges and needn't reach their ends.
There are 2 independent parts, one for each index of `groups`. The reference program is written for one: setup_inputs(seed, part) draws one part's arguments, and reference() takes and returns one part's arrays. A program takes and returns all parts, laid end to end along the dimension named above; each array names one. Nothing has to cross between parts.
Inputs may be any that keep to these rules, and one draw needn't show every extreme that they name: Each request has at least one block, the lengths sum to 32, and the longest request has exactly 12 blocks. Request r and request r + 4 together have at most 16 blocks, exactly so for the pair of the longest request. `row_positions`: each request's positions are non-decreasing and lie below 256 times its length; its last recomputed row is its last token, 256 lengths[r] - 1. `block_order`: A permutation; the 2 slots of one device (slots 2 d to 2 d + 1) hold blocks of requests r1, r2 with r1 % (4) != r2 % 4.
All inputs are finite; a program needn't handle non-finite values.
Results may differ from the reference program's by a relative error of at most 0.0041.
Values may be sent and summed in bfloat16 or wider, within the bound.
No kernel may reach another device: no remote copies, remote signals or barrier semaphores. Data moves between devices by JAX's collectives and lax.ppermute only.
A program may use at most 64 MiB of HBM per device.

```python
import math
import jax
import jax.numpy as jnp
from jax import lax

QH = 64
KVH = 8
HD = 128
BLOCK = 256
REQS = 8
ROWS_REQ = 128
NB = 32
MOST = 12


def query_base(base_key):
    normal_key = jax.random.fold_in(base_key, 501)
    drawn = jnp.clip(jax.random.normal(normal_key, (ROWS_REQ, REQS, KVH, QH // KVH, HD), jnp.float32), -6.0, 6.0)
    return drawn


def length_table(base_key):
    table_key = jax.random.fold_in(base_key, 701)
    longest_key = jax.random.fold_in(table_key, 1)
    split_key = jax.random.fold_in(table_key, 2)
    flip_key = jax.random.fold_in(table_key, 3)
    half_reqs = REQS // 2
    others = half_reqs - 1
    longest = jax.random.randint(longest_key, (), 0, REQS)
    long_pair = longest % half_reqs
    rest = NB - NB // 2
    pair_ids = jnp.arange(half_reqs, dtype=jnp.int32)
    rank = pair_ids - (pair_ids > long_pair).astype(jnp.int32)
    totals = rest // others + (rank < rest % others).astype(jnp.int32)
    first = jax.random.randint(split_key, (half_reqs,), 1, totals)
    flips = jax.random.randint(flip_key, (half_reqs,), 0, 2)
    low_len = jnp.where(flips == 1, first, totals - first)
    high_len = totals - low_len
    partner_len = NB // 2 - MOST
    long_low = jnp.where(longest < half_reqs, MOST, partner_len)
    long_high = jnp.where(longest < half_reqs, partner_len, MOST)
    low_len = jnp.where(pair_ids == long_pair, long_low, low_len)
    high_len = jnp.where(pair_ids == long_pair, long_high, high_len)
    return jnp.concatenate([low_len, high_len]).astype(jnp.int32)


def draw_lengths(key, part):
    return length_table(key)


def draw_block_order(key, part):
    table = length_table(key)
    starts = jnp.cumsum(table) - table
    block_ids = jnp.arange(NB, dtype=jnp.int32)
    req_of = jnp.sum((block_ids[:, None] >= starts[None, 1:]).astype(jnp.int32), axis=1)
    pair_of = req_of % (REQS // 2)
    ranks = jax.random.permutation(jax.random.fold_in(key, 801), NB).astype(jnp.int32)
    sorted_ids = jnp.argsort(pair_of * NB + ranks, stable=True).astype(jnp.int32)
    holders = NB // 2
    device_perm = jax.random.permutation(jax.random.fold_in(key, 802), holders).astype(jnp.int32)
    swapped = jax.random.randint(jax.random.fold_in(key, 803), (holders,), 0, 2)
    slot_pick = jnp.arange(2, dtype=jnp.int32)
    flipped = jnp.abs(slot_pick[None, :] - swapped[:, None])
    places = device_perm[:, None] + holders * flipped
    return sorted_ids[places.reshape(NB)].astype(jnp.int32)


def draw_row_positions(key, part):
    table = length_table(key)
    pick_key = jax.random.fold_in(key, 702)
    last_row = BLOCK * table - 1
    picks = jax.random.randint(pick_key, (REQS, ROWS_REQ - 1), 0, last_row[:, None])
    picks = jnp.sort(picks, axis=1)
    return jnp.concatenate([picks, last_row[:, None]], axis=1).astype(jnp.int32)


def draw_queries(key, part):
    return query_base(key).reshape(ROWS_REQ, REQS * QH * HD).astype(jnp.bfloat16)


def draw_fresh_rows(key, part):
    drawn = query_base(key)
    noise_key = jax.random.fold_in(key, 503)
    value_key = jax.random.fold_in(key, 504)
    noise = jnp.clip(jax.random.normal(noise_key, (ROWS_REQ, REQS, KVH, HD), jnp.float32), -6.0, 6.0)
    fresh_keys = 0.7 * jnp.sum(drawn, axis=3) + 0.5 * noise
    fresh_values = jnp.clip(jax.random.normal(value_key, (ROWS_REQ, REQS, KVH, HD), jnp.float32), -6.0, 6.0)
    stacked = jnp.stack([fresh_keys, fresh_values], axis=3)
    return stacked.reshape(ROWS_REQ, REQS * KVH * 2 * HD).astype(jnp.bfloat16)


def level_of(rng, shape, split, least, largest):
    factor_of, own = 1.0, jax.random.fold_in(rng, 6)
    for position, shards_of in split:
        heights = jnp.exp(jax.random.uniform(jax.random.fold_in(own, position), (shards_of,), jnp.float32, least / len(split), largest / len(split)))
        factor_of = factor_of * jnp.repeat(heights, shape[position] // shards_of).reshape([-1 if axis == position else 1 for axis in range(len(shape))])
    return factor_of


def scatter_about(stream_key, shape, width, reach, shards=(), kind=jnp.bfloat16):
    entries = jax.random.normal(stream_key, shape, jnp.float32) * width
    if len(shards) > 0:
        entries = level_of(stream_key, shape, shards, -0.22, 0.18) * entries
    return jnp.clip(entries, min=-reach, max=reach).astype(kind)


def setup_inputs(seed: int = 0, part: int = 0) -> dict:
    key_of = jax.random.split(jax.random.key(seed), 7)
    part_splits = jax.random.split(jax.random.fold_in(key_of[6], part), 7)
    kv_store = scatter_about(part_splits[0], (NB, BLOCK, 2 * KVH * HD), 1.0, 6.0, ((0, 16),))
    block_order = draw_block_order(jax.random.fold_in(jax.random.fold_in(key_of[6], part), 71), part)
    lengths = draw_lengths(jax.random.fold_in(jax.random.fold_in(key_of[6], part), 71), part)
    row_positions = draw_row_positions(jax.random.fold_in(jax.random.fold_in(key_of[6], part), 71), part)
    queries = draw_queries(jax.random.fold_in(jax.random.fold_in(key_of[6], part), 71), part)
    fresh_rows = draw_fresh_rows(jax.random.fold_in(jax.random.fold_in(key_of[6], part), 71), part)
    return {"kv_store": kv_store, "block_order": block_order, "lengths": lengths, "row_positions": row_positions, "queries": queries, "fresh_rows": fresh_rows}


ROPE_BASE = 500000.0
NEG_FILL = -1e+30

def frequencies(half_size):
    step_ids = jnp.arange(half_size, dtype=jnp.float32)
    return jnp.exp(-math.log(ROPE_BASE) * step_ids / half_size)

def rotate(vectors, turn_angle):
    half_size = vectors.shape[-1] // 2
    cosine = jnp.cos(turn_angle)
    sine_part = jnp.sin(turn_angle)
    lower_half = vectors[..., :half_size]
    upper_half = vectors[..., half_size:]
    return jnp.concatenate([lower_half * cosine - upper_half * sine_part, upper_half * cosine + lower_half * sine_part], axis=-1)

def round_trip(values):
    return lax.optimization_barrier(values.astype(jnp.bfloat16)).astype(jnp.float32)

def merge_state(acc_state, block_term):
    old_top, old_sum, old_out = acc_state
    new_top, new_sum, new_out = block_term
    joined_top = jnp.maximum(old_top, new_top)
    old_factor = jnp.exp(old_top - joined_top)
    new_factor = jnp.exp(new_top - joined_top)
    return (joined_top, old_sum * old_factor + new_sum * new_factor, old_out * old_factor[..., None] + new_out * new_factor[..., None])

def reference_partial(query_set, row_limit, key_block, value_block, offset, score_scale):
    scores = jnp.einsum('ncgd,tcd->cgnt', query_set, key_block) * score_scale
    key_positions = offset + jnp.arange(key_block.shape[0], dtype=jnp.int32)
    allowed = key_positions[None, :] < row_limit[:, None]
    block_top = lax.optimization_barrier(jnp.max(jnp.where(allowed, scores, NEG_FILL), axis=-1))
    weights = round_trip(jnp.where(allowed, jnp.exp(scores - block_top[..., None]), 0.0))
    weight_sum = lax.optimization_barrier(jnp.sum(weights, axis=-1))
    summed = jnp.einsum('cgnt,tcd->cgnd', weights, value_block)
    return (block_top, weight_sum, summed)

def reference(kv_store, block_order, lengths, row_positions, queries, fresh_rows):
    group_size = QH // KVH
    score_scale = 1.0 / math.sqrt(HD)
    frequency = frequencies(HD // 2)
    lengths = lengths.astype(jnp.int32)
    starts = (jnp.cumsum(lengths) - lengths).astype(jnp.int32)
    block_ids = jnp.arange(NB, dtype=jnp.int32)
    inverse = jnp.zeros((NB,), jnp.int32).at[block_order.astype(jnp.int32)].set(block_ids)
    req_of = lax.optimization_barrier(jnp.sum((block_ids[:, None] >= starts[None, 1:]).astype(jnp.int32), axis=1)).astype(jnp.int32)
    pos_of = (block_ids - starts[req_of]).astype(jnp.int32)
    row_limits = row_positions.astype(jnp.int32)
    row_angle = jnp.transpose(row_limits).astype(jnp.float32)[..., None] * frequency
    query_f32 = queries.reshape(ROWS_REQ, REQS, KVH, group_size, HD).astype(jnp.float32)
    rotated_q = round_trip(rotate(query_f32, row_angle[:, :, None, None, :]))
    fresh_split = fresh_rows.reshape(ROWS_REQ, REQS, KVH, 2, HD)
    own_key = round_trip(rotate(fresh_split[:, :, :, 0].astype(jnp.float32), row_angle[:, :, None, :]))
    own_value = fresh_split[:, :, :, 1].astype(jnp.float32)
    own_score = jnp.einsum('nrcgd,nrcd->rcgn', rotated_q, own_key) * score_scale
    own_out = jnp.broadcast_to(jnp.transpose(own_value, (1, 2, 0, 3))[:, :, None], (REQS, KVH, group_size, ROWS_REQ, HD))
    start_state = (own_score, jnp.ones_like(own_score), own_out)
    query_by_req = jnp.transpose(rotated_q, (1, 0, 2, 3, 4))

    def one_block(carried, block_id):
        slot_id = inverse[block_id]
        request = req_of[block_id]
        offset = pos_of[block_id] * BLOCK
        block_kv = lax.dynamic_index_in_dim(kv_store, slot_id, 0, keepdims=False).reshape(BLOCK, KVH, 2, HD)
        key_block = round_trip(rotate(block_kv[:, :, 0].astype(jnp.float32), offset.astype(jnp.float32) * frequency))
        query_set = lax.dynamic_index_in_dim(query_by_req, request, 0, keepdims=False)
        row_limit = lax.dynamic_index_in_dim(row_limits, request, 0, keepdims=False)
        block_term = reference_partial(query_set, row_limit, key_block, block_kv[:, :, 1].astype(jnp.float32), offset, score_scale)
        older = tuple((lax.dynamic_index_in_dim(member, request, 0, keepdims=False) for member in carried))
        joined = merge_state(older, block_term)
        carried = tuple((lax.dynamic_update_index_in_dim(whole, piece, request, 0) for whole, piece in zip(carried, joined)))
        return (carried, None)
    final_state, unused = lax.scan(one_block, start_state, block_ids)
    normalized = final_state[2] / final_state[1][..., None]
    return jnp.transpose(normalized, (3, 0, 1, 2, 4)).reshape(ROWS_REQ, REQS * QH * HD).astype(jnp.bfloat16)
```

```python
import functools
import math

import jax
import jax.numpy as jnp
import numpy as np
from jax import lax
from jax.experimental import pallas as pl
from jax.experimental.pallas import tpu as pltpu
from jax.sharding import PartitionSpec as P

HD = 128
ROPE_BASE = 500000.0
TOP_START = -1e30
MASKED = -3e30
STATS = 16


VMEM = pltpu.MemorySpace.VMEM
SMEM = pltpu.MemorySpace.SMEM


def frequency_row():
    half = HD // 2
    steps = np.arange(half, dtype=np.float32)
    row = np.exp((-math.log(ROPE_BASE) * steps / half).astype(np.float32)).astype(np.float32)
    return np.concatenate([row, row])[None, :]


def signed(sine):
    lane = lax.broadcasted_iota(jnp.int32, sine.shape, len(sine.shape) - 1)
    return jnp.where(lane < HD // 2, -sine, sine)


def turn(vectors, cosine, sine):
    wide = vectors.astype(jnp.float32)
    return (wide * cosine + pltpu.roll(wide, HD // 2, 1) * sine).astype(jnp.bfloat16)


def find_block(block_id, lengths_ref):
    start = jnp.int32(0)
    request = jnp.int32(0)
    position = jnp.int32(0)
    for q in range(lengths_ref.shape[0]):
        end = start + lengths_ref[q]
        inside = (block_id >= start) & (block_id < end)
        request = jnp.where(inside, q, request)
        position = jnp.where(inside, block_id - start, position)
        start = end
    return request, position


def pack_kv(n_sub, order_ref, lengths_ref, freq_ref, kv_ref, *out_refs):
    heads = len(out_refs)
    my_head = lax.axis_index("shard") // n_sub
    block_len = kv_ref.shape[1]
    unused, position = find_block(order_ref[pl.program_id(0)], lengths_ref)
    angle = (position * block_len).astype(jnp.float32) * freq_ref[...]
    cosine, sine = jnp.cos(angle), signed(jnp.sin(angle))
    for mask in range(heads):
        column = pl.multiple_of((my_head ^ mask) * (2 * HD), 2 * HD)
        out_refs[mask][0, :, :HD] = turn(kv_ref[0, :, pl.ds(column, HD)], cosine, sine)
        out_refs[mask][0, :, HD:] = kv_ref[0, :, pl.ds(column + HD, HD)]


def pack_queries(n_sub, group_size, freq_ref, rows_ref, queries_ref, fresh_ref, *refs):
    out_refs, key_ref, cos_ref, sin_ref = refs[:-3], refs[-3], refs[-2], refs[-1]
    request = lax.axis_index("shard") // n_sub
    rows = queries_ref.shape[0]
    kv_local = fresh_ref.shape[1] // (2 * HD)
    sub_heads = group_size // n_sub
    angle = rows_ref[...].astype(jnp.float32) * freq_ref[...]
    cos_ref[...] = jnp.cos(angle)
    sin_ref[...] = signed(jnp.sin(angle))
    for kv_id in range(kv_local):
        key_ref[kv_id] = turn(fresh_ref[:, 2 * kv_id * HD : (2 * kv_id + 1) * HD], cos_ref[...], sin_ref[...])
    for step, out_ref in enumerate(out_refs):
        kv_id = (step % kv_local) ^ (request % kv_local)
        sub = (step // kv_local) ^ (request // kv_local)
        for head in range(sub_heads):
            column = pl.multiple_of((kv_id * group_size + sub * sub_heads + head) * HD, HD)
            out_ref[head * rows : (head + 1) * rows, :] = turn(
                queries_ref[:, pl.ds(column, HD)], cos_ref[...], sin_ref[...]
            )


def attend(n_sub, buffers, first, last, blk_dev, order_ref, lengths_ref, rows_ref, *refs):
    n_req = lengths_ref.shape[0]
    n_buf = len(buffers)
    query_refs, refs = refs[:n_req], refs[n_req:]
    kv_refs, refs = refs[:n_buf], refs[n_buf:]
    if not first:
        acc_in, top_in, refs = refs[0], refs[1], refs[2:]
    if last:
        out_refs, refs = refs[:n_req], refs[n_req:]
        acc_ref, top_ref, refs = refs[0], refs[1], refs[2:]
    else:
        acc_ref, top_ref, refs = refs[0], refs[1], refs[2:]
    query_buf, kv_buf, id_ref, query_sem, kv_sem = refs
    query_copies = [pltpu.make_async_copy(ref, query_buf.at[i], query_sem.at[i]) for i, ref in enumerate(query_refs)]
    kv_copies = [
        pltpu.make_async_copy(ref, kv_buf.at[pl.ds(i * blk_dev, blk_dev)], kv_sem.at[i]) for i, ref in enumerate(kv_refs)
    ]
    for copy in query_copies + kv_copies:
        copy.start()
    me = lax.axis_index("shard")
    my_head, my_sub = me // n_sub, me % n_sub
    kv_local = n_req // n_sub
    mixed = my_sub * kv_local + my_head % kv_local
    block_len = kv_buf.shape[1]
    width = rows_ref.shape[2]
    for i, (mask, back) in enumerate(buffers):
        device = (my_head ^ mask) * n_sub + lax.rem(my_sub - back + n_sub, n_sub)
        for slot in range(blk_dev):
            id_ref[i * blk_dev + slot] = order_ref[device * blk_dev + slot]
    if first:
        acc_ref[...] = jnp.zeros_like(acc_ref)
        top_ref[...] = jnp.full_like(top_ref, TOP_START)
    else:
        acc_ref[...] = acc_in[...]
        top_ref[...] = top_in[...]
    for copy in query_copies + kv_copies:
        copy.wait()
    scale = math.log2(math.e) / math.sqrt(HD)
    token = lax.broadcasted_iota(jnp.int32, (block_len, width), 0)

    def one_block(i, carried):
        request, position = find_block(id_ref[i], lengths_ref)
        scores = lax.dot_general(
            kv_buf[i, :, :HD],
            query_buf[request ^ mixed],
            (((1,), (1,)), ((), ())),
            preferred_element_type=jnp.float32,
        )
        limit = rows_ref[request] - position * block_len
        scores = jnp.where(token < limit, scores * scale, MASKED)
        old_top = top_ref[request]
        new_top = jnp.maximum(old_top, jnp.max(scores, axis=0, keepdims=True))
        factor = jnp.exp2(old_top - new_top)
        weights = jnp.exp2(scores - new_top).astype(jnp.bfloat16)
        values = jnp.concatenate(
            [jnp.transpose(kv_buf[i, :, HD:]), jnp.ones((STATS, block_len), jnp.bfloat16)], axis=0
        )
        summed = jnp.dot(values, weights, preferred_element_type=jnp.float32)
        acc_ref[request] = acc_ref[request] * factor + summed[: HD + 8]
        top_ref[request] = new_top
        return carried

    lax.fori_loop(0, n_buf * blk_dev, one_block, 0)

    if last:
        sub_heads = width // HD
        for step, out_ref in enumerate(out_refs):
            request = step ^ mixed
            total = acc_ref[request, HD : HD + 1]
            some = total > 0.0
            result = acc_ref[request, :HD] / jnp.where(some, total, 1.0)
            level = jnp.where(some, top_ref[request] + jnp.log2(jnp.where(some, total, 1.0)), TOP_START)
            for head in range(sub_heads):
                lanes = slice(head * HD, (head + 1) * HD)
                out_ref[lanes, :] = jnp.transpose(result[:, lanes]).astype(jnp.bfloat16)
            level = jnp.concatenate([level[:, head * HD : (head + 1) * HD] for head in range(sub_heads)], axis=0)
            high = level.astype(jnp.bfloat16)
            rest = level - high.astype(jnp.float32)
            middle = rest.astype(jnp.bfloat16)
            low = (rest - middle.astype(jnp.float32)).astype(jnp.bfloat16)
            pieces = [high, middle, low, jnp.zeros((STATS - 3 * sub_heads, HD), jnp.bfloat16)]
            out_ref[width : width + STATS, :] = jnp.concatenate(pieces, axis=0)


def merge_own(n_sub, group_size, key_ref, fresh_ref, *refs):
    steps = (len(refs) - 2) // 2
    query_refs, part_refs, out_ref, level_ref = refs[:steps], refs[steps : 2 * steps], refs[-2], refs[-1]
    request = lax.axis_index("shard") // n_sub
    rows = out_ref.shape[0]
    kv_local = key_ref.shape[0]
    sub_heads = group_size // n_sub
    scale = math.log2(math.e) / math.sqrt(HD)
    level_ref[...] = jnp.zeros_like(level_ref)
    for step in range(steps):
        stats = part_refs[step][sub_heads * rows :, :].astype(jnp.float32)
        level_ref[step * sub_heads : (step + 1) * sub_heads] = (
            stats[:sub_heads] + stats[sub_heads : 2 * sub_heads] + stats[2 * sub_heads : 3 * sub_heads]
        )
    levels = jnp.transpose(level_ref[...])
    for step in range(steps):
        kv_id = (step % kv_local) ^ (request % kv_local)
        sub = (step // kv_local) ^ (request // kv_local)
        own_key = key_ref[kv_id].astype(jnp.float32)
        value_column = pl.multiple_of((2 * kv_id + 1) * HD, HD)
        own_value = fresh_ref[:, pl.ds(value_column, HD)].astype(jnp.float32)
        for head in range(sub_heads):
            part = slice(head * rows, (head + 1) * rows)
            query = query_refs[step][part, :].astype(jnp.float32)
            own = jnp.sum(query * own_key, axis=1, keepdims=True) * scale
            level = levels[:, step * sub_heads + head : step * sub_heads + head + 1]
            top = jnp.maximum(own, level)
            own_weight = jnp.exp2(own - top)
            weight = jnp.exp2(level - top)
            share = 1.0 / (own_weight + weight)
            column = pl.multiple_of((kv_id * group_size + sub * sub_heads + head) * HD, HD)
            out_ref[:, pl.ds(column, HD)] = (
                part_refs[step][part, :].astype(jnp.float32) * (weight * share) + own_value * (own_weight * share)
            ).astype(jnp.bfloat16)


def shards(kv_store, block_order, lengths, row_positions, queries, fresh_rows):
    n_shard = lax.axis_size("shard")
    n_req, rows = row_positions.shape
    n_sub = n_shard // n_req
    blk_dev, block_len, full_width = kv_store.shape
    kv_heads = full_width // (2 * HD)
    kv_local = kv_heads // n_sub
    group_size = queries.shape[1] // (kv_local * HD)
    sub_heads = group_size // n_sub
    width = sub_heads * rows
    bf16 = jnp.bfloat16
    freq = jnp.asarray(frequency_row())
    spec = functools.partial(pl.BlockSpec, memory_space=VMEM)
    smem = pl.BlockSpec(memory_space=SMEM)
    anywhere = pl.BlockSpec(memory_space=pl.ANY)

    my_rows = lax.dynamic_index_in_dim(row_positions, lax.axis_index("shard") // n_sub, 0, keepdims=False)
    packed = pl.pallas_call(
        functools.partial(pack_queries, n_sub, group_size),
        out_shape=[jax.ShapeDtypeStruct((width, HD), bf16)] * n_req + [jax.ShapeDtypeStruct((kv_local, rows, HD), bf16)],
        in_specs=[spec()] * 4,
        out_specs=[spec()] * (n_req + 1),
        scratch_shapes=[pltpu.VMEM((rows, HD), jnp.float32)] * 2,
        name="pack_queries",
    )(freq, my_rows[:, None], queries, fresh_rows)
    sent_queries, own_key = packed[:n_req], packed[n_req]

    packed_kv = pl.pallas_call(
        functools.partial(pack_kv, n_sub),
        grid=(blk_dev,),
        out_shape=[jax.ShapeDtypeStruct((blk_dev, block_len, 2 * HD), bf16)] * kv_heads,
        in_specs=[smem, smem, pl.BlockSpec((1, HD), lambda i: (0, 0)), pl.BlockSpec((1, block_len, full_width), lambda i: (i, 0, 0))],
        out_specs=[pl.BlockSpec((1, block_len, 2 * HD), lambda i: (i, 0, 0))] * kv_heads,
        name="pack_kv",
    )(block_order, lengths, freq, kv_store)

    to_compute = []
    for step in range(n_req):
        pairs = []
        for request in range(n_req):
            for h in range(n_sub):
                head = kv_local * h + ((step % kv_local) ^ (request % kv_local))
                sub = (step // kv_local) ^ (request // kv_local)
                pairs.append((request * n_sub + h, head * n_sub + sub))
        to_compute.append(pairs)
    held_queries = [lax.ppermute(x, "shard", pairs) for x, pairs in zip(sent_queries, to_compute)]

    all_order = lax.all_gather(block_order, "shard", axis=0, tiled=True)
    wide_rows = jnp.tile(row_positions, (1, sub_heads))[:, None, :]

    def at_head(mask):
        pairs = [(d, ((d // n_sub) ^ mask) * n_sub + d % n_sub) for d in range(n_shard)]
        return packed_kv[mask] if mask == 0 else lax.ppermute(packed_kv[mask], "shard", pairs)

    def from_sub(x, back):
        pairs = [(d, (d // n_sub) * n_sub + (d % n_sub + back) % n_sub) for d in range(n_shard)]
        return x if back == 0 else lax.ppermute(x, "shard", pairs)

    far_first = list(range(kv_heads // 2, kv_heads))
    landed = {mask: at_head(mask) for mask in far_first}
    landed.update({mask: at_head(mask) for mask in range(kv_heads // 2)})
    groups = [list(range(kv_heads // 2)), far_first]
    state_shapes = [
        jax.ShapeDtypeStruct((n_req, HD + 8, width), jnp.float32),
        jax.ShapeDtypeStruct((n_req, 1, width), jnp.float32),
    ]
    part_shapes = [jax.ShapeDtypeStruct((width + STATS, HD), bf16)] * n_req
    state = []
    for index, masks in enumerate(groups):
        buffers = [(mask, back) for mask in masks for back in range(n_sub)]
        first, last = index == 0, index == len(groups) - 1
        blocks = len(buffers) * blk_dev
        results = pl.pallas_call(
            functools.partial(attend, n_sub, buffers, first, last, blk_dev),
            out_shape=part_shapes if last else state_shapes,
            in_specs=[smem, smem, spec()] + [anywhere] * (n_req + len(buffers)) + [spec()] * len(state),
            out_specs=[spec()] * (n_req if last else 2),
            scratch_shapes=([pltpu.VMEM(s.shape, s.dtype) for s in state_shapes] if last else [])
            + [
                pltpu.VMEM((n_req, width, HD), bf16),
                pltpu.VMEM((blocks, block_len, 2 * HD), bf16),
                pltpu.SMEM((blocks,), jnp.int32),
                pltpu.SemaphoreType.DMA((n_req,)),
                pltpu.SemaphoreType.DMA((len(buffers),)),
            ],
            name=f"attend_{index}",
        )(all_order, lengths, wide_rows, *held_queries, *[from_sub(landed[mask], back) for mask, back in buffers], *state)
        state = list(results)
    returned = []
    for part, pairs in zip(state, to_compute):
        returned.append(lax.ppermute(part, "shard", [(b, a) for a, b in pairs]))

    return pl.pallas_call(
        functools.partial(merge_own, n_sub, group_size),
        out_shape=jax.ShapeDtypeStruct((rows, kv_local * group_size * HD), bf16),
        in_specs=[spec()] * (2 + 2 * n_req),
        out_specs=spec(),
        scratch_shapes=[pltpu.VMEM((max(HD, n_req * sub_heads), rows), jnp.float32)],
        name="merge_own",
    )(own_key, fresh_rows, *sent_queries, *returned)


def solution(mesh):
    in_specs = (
        P(("groups", "shard"), None, None),
        P(("groups", "shard")),
        P("groups"),
        P("groups", None),
        P("groups", "shard"),
        P("groups", "shard"),
    )
    return jax.shard_map(shards, mesh=mesh, in_specs=in_specs, out_specs=P("groups", "shard"), check_vma=False)
```

```python
import functools
import math

import jax
import jax.numpy as jnp
import numpy as np
from jax import lax
from jax.experimental import pallas as pl
from jax.experimental.pallas import tpu as pltpu
from jax.sharding import PartitionSpec as P


HD = 128
ROPE_BASE = 500000.0
TOP_START = -1e30
MASKED = -3e30
STATS = 16
TAG = 8


VMEM = pltpu.MemorySpace.VMEM
SMEM = pltpu.MemorySpace.SMEM


def frequency_row():
    half = HD // 2
    steps = np.arange(half, dtype=np.float32)
    row = np.exp((-math.log(ROPE_BASE) * steps / half).astype(np.float32)).astype(np.float32)
    return np.concatenate([row, row])[None, :]


def signed(sine):
    lane = lax.broadcasted_iota(jnp.int32, sine.shape, len(sine.shape) - 1)
    return jnp.where(lane < HD // 2, -sine, sine)


def turn(vectors, cosine, sine):
    wide = vectors.astype(jnp.float32)
    return (wide * cosine + pltpu.roll(wide, HD // 2, 1) * sine).astype(jnp.bfloat16)


def find_block(block_id, lengths_ref):
    start = jnp.int32(0)
    request = jnp.int32(0)
    position = jnp.int32(0)
    for q in range(lengths_ref.shape[0]):
        end = start + lengths_ref[q]
        inside = (block_id >= start) & (block_id < end)
        request = jnp.where(inside, q, request)
        position = jnp.where(inside, block_id - start, position)
        start = end
    return request, position


def pack_kv(n_sub, order_ref, lengths_ref, freq_ref, kv_ref, *out_refs):
    heads = len(out_refs)
    my_head = lax.axis_index("shard") // n_sub
    block_len = kv_ref.shape[1]
    block_id = order_ref[pl.program_id(0)]
    _, position = find_block(block_id, lengths_ref)
    angle = (position * block_len).astype(jnp.float32) * freq_ref[...]
    cosine, sine = jnp.cos(angle), signed(jnp.sin(angle))
    for mask in range(heads):
        column = pl.multiple_of((my_head ^ mask) * (2 * HD), 2 * HD)
        out_refs[mask][0, :block_len, :HD] = turn(kv_ref[0, :, pl.ds(column, HD)], cosine, sine)
        out_refs[mask][0, :block_len, HD:] = kv_ref[0, :, pl.ds(column + HD, HD)]
        out_refs[mask][0, block_len:, :] = jnp.full((TAG, 2 * HD), block_id, jnp.int32).astype(jnp.float32).astype(jnp.bfloat16)


def pack_queries(n_sub, group_size, freq_ref, rows_ref, queries_ref, fresh_ref, *refs):
    out_refs, key_ref, cos_ref, sin_ref = refs[:-3], refs[-3], refs[-2], refs[-1]
    request = lax.axis_index("shard") // n_sub
    rows = queries_ref.shape[0]
    kv_local = fresh_ref.shape[1] // (2 * HD)
    sub_heads = group_size // n_sub
    position = rows_ref[pl.ds(request, 1), :].astype(jnp.float32)
    angle = jnp.transpose(jnp.broadcast_to(position, (HD, rows))) * freq_ref[...]
    cos_ref[...] = jnp.cos(angle)
    sin_ref[...] = signed(jnp.sin(angle))
    for kv_id in range(kv_local):
        key_ref[kv_id] = turn(fresh_ref[:, 2 * kv_id * HD : (2 * kv_id + 1) * HD], cos_ref[...], sin_ref[...])
    for step, out_ref in enumerate(out_refs):
        kv_id = (step % kv_local) ^ (request % kv_local)
        sub = (step // kv_local) ^ (request // kv_local)
        for head in range(sub_heads):
            column = pl.multiple_of((kv_id * group_size + sub * sub_heads + head) * HD, HD)
            out_ref[head * rows : (head + 1) * rows, :] = turn(
                queries_ref[:, pl.ds(column, HD)], cos_ref[...], sin_ref[...]
            )


def attend(n_sub, n_buf, first, last, blk_dev, lengths_ref, rows_ref, *refs):
    n_req = lengths_ref.shape[0]
    query_refs, refs = refs[:n_req], refs[n_req:]
    kv_refs, refs = refs[:n_buf], refs[n_buf:]
    if not first:
        acc_in, top_in, refs = refs[0], refs[1], refs[2:]
    if last:
        out_refs, refs = refs[:n_req], refs[n_req:]
        acc_ref, top_ref, refs = refs[0], refs[1], refs[2:]
    else:
        acc_ref, top_ref, refs = refs[0], refs[1], refs[2:]
    query_buf, kv_buf, id_ref, query_sem, kv_sem = refs
    query_copies = [pltpu.make_async_copy(ref, query_buf.at[i], query_sem.at[i]) for i, ref in enumerate(query_refs)]
    kv_copies = [
        pltpu.make_async_copy(ref, kv_buf.at[pl.ds(i * blk_dev, blk_dev)], kv_sem.at[i]) for i, ref in enumerate(kv_refs)
    ]
    for copy in query_copies + kv_copies:
        copy.start()
    me = lax.axis_index("shard")
    my_head, my_sub = me // n_sub, me % n_sub
    kv_local = n_req // n_sub
    mixed = my_sub * kv_local + my_head % kv_local
    block_len = kv_buf.shape[1] - TAG
    width = rows_ref.shape[2]
    if first:
        acc_ref[...] = jnp.zeros_like(acc_ref)
        top_ref[...] = jnp.full_like(top_ref, TOP_START)
    else:
        acc_ref[...] = acc_in[...]
        top_ref[...] = top_in[...]
    for copy in query_copies + kv_copies:
        copy.wait()
    for i in range(n_buf * blk_dev):
        id_ref[i] = jnp.max(kv_buf[i, block_len:, :].astype(jnp.float32)).astype(jnp.int32)
    scale = math.log2(math.e) / math.sqrt(HD)
    token = lax.broadcasted_iota(jnp.int32, (block_len, width), 0)

    def one_block(i, carried):
        request, position = find_block(id_ref[i], lengths_ref)
        scores = lax.dot_general(
            kv_buf[i, :block_len, :HD],
            query_buf[request ^ mixed],
            (((1,), (1,)), ((), ())),
            preferred_element_type=jnp.float32,
        )
        limit = rows_ref[request] - position * block_len
        scores = jnp.where(token < limit, scores * scale, MASKED)
        old_top = top_ref[request]
        new_top = jnp.maximum(old_top, jnp.max(scores, axis=0, keepdims=True))
        factor = jnp.exp2(old_top - new_top)
        weights = jnp.exp2(scores - new_top).astype(jnp.bfloat16)
        values = jnp.concatenate(
            [jnp.transpose(kv_buf[i, :block_len, HD:]), jnp.ones((STATS, block_len), jnp.bfloat16)], axis=0
        )
        summed = jnp.dot(values, weights, preferred_element_type=jnp.float32)
        acc_ref[request] = acc_ref[request] * factor + summed[: HD + 8]
        top_ref[request] = new_top
        return carried

    lax.fori_loop(0, n_buf * blk_dev, one_block, 0)

    if last:
        sub_heads = width // HD
        for step, out_ref in enumerate(out_refs):
            request = step ^ mixed
            total = acc_ref[request, HD : HD + 1]
            some = total > 0.0
            result = acc_ref[request, :HD] / jnp.where(some, total, 1.0)
            level = jnp.where(some, top_ref[request] + jnp.log2(jnp.where(some, total, 1.0)), TOP_START)
            for head in range(sub_heads):
                lanes = slice(head * HD, (head + 1) * HD)
                out_ref[lanes, :] = jnp.transpose(result[:, lanes]).astype(jnp.bfloat16)
            level = jnp.concatenate([level[:, head * HD : (head + 1) * HD] for head in range(sub_heads)], axis=0)
            high = level.astype(jnp.bfloat16)
            rest = level - high.astype(jnp.float32)
            middle = rest.astype(jnp.bfloat16)
            low = (rest - middle.astype(jnp.float32)).astype(jnp.bfloat16)
            pieces = [high, middle, low, jnp.zeros((STATS - 3 * sub_heads, HD), jnp.bfloat16)]
            out_ref[width : width + STATS, :] = jnp.concatenate(pieces, axis=0)


def own_scores(n_sub, group_size, key_ref, *refs):
    query_refs, own_ref = refs[:-1], refs[-1]
    request = lax.axis_index("shard") // n_sub
    kv_local, rows = key_ref.shape[:2]
    sub_heads = group_size // n_sub
    scale = math.log2(math.e) / math.sqrt(HD)
    own_ref[...] = jnp.zeros_like(own_ref)
    for step, query_ref in enumerate(query_refs):
        own_key = key_ref[(step % kv_local) ^ (request % kv_local)].astype(jnp.float32)
        for head in range(sub_heads):
            query = query_ref[head * rows : (head + 1) * rows, :].astype(jnp.float32)
            column = step * sub_heads + head
            own_ref[:, column : column + 1] = jnp.sum(query * own_key, axis=1, keepdims=True) * scale


def merge_own(n_sub, group_size, own_ref, fresh_ref, *refs):
    part_refs, out_ref, level_ref = refs[:-2], refs[-2], refs[-1]
    request = lax.axis_index("shard") // n_sub
    rows = out_ref.shape[0]
    kv_local = fresh_ref.shape[1] // (2 * HD)
    sub_heads = group_size // n_sub
    level_ref[...] = jnp.zeros_like(level_ref)
    for step, part_ref in enumerate(part_refs):
        stats = part_ref[sub_heads * rows :, :].astype(jnp.float32)
        level_ref[step * sub_heads : (step + 1) * sub_heads] = (
            stats[:sub_heads] + stats[sub_heads : 2 * sub_heads] + stats[2 * sub_heads : 3 * sub_heads]
        )
    level = jnp.transpose(level_ref[...])
    own = own_ref[...]
    top = jnp.maximum(own, level)
    own_share = jnp.exp2(own - top)
    share = jnp.exp2(level - top)
    norm = 1.0 / (own_share + share)
    own_share, share = own_share * norm, share * norm
    for step, part_ref in enumerate(part_refs):
        kv_id = (step % kv_local) ^ (request % kv_local)
        sub = (step // kv_local) ^ (request // kv_local)
        value_column = pl.multiple_of((2 * kv_id + 1) * HD, HD)
        own_value = fresh_ref[:, pl.ds(value_column, HD)].astype(jnp.float32)
        for head in range(sub_heads):
            lane = step * sub_heads + head
            part = part_ref[head * rows : (head + 1) * rows, :].astype(jnp.float32)
            column = pl.multiple_of((kv_id * group_size + sub * sub_heads + head) * HD, HD)
            out_ref[:, pl.ds(column, HD)] = (
                part * share[:, lane : lane + 1] + own_value * own_share[:, lane : lane + 1]
            ).astype(jnp.bfloat16)


def moved(x, pairs):
    return lax.ppermute(x, "shard", pairs)


def shards(kv_store, block_order, lengths, row_positions, queries, fresh_rows):
    n_shard = lax.axis_size("shard")
    n_req, rows = row_positions.shape
    n_sub = n_shard // n_req
    blk_dev, block_len, full_width = kv_store.shape
    kv_heads = full_width // (2 * HD)
    kv_local = kv_heads // n_sub
    group_size = queries.shape[1] // (kv_local * HD)
    sub_heads = group_size // n_sub
    width = sub_heads * rows
    bf16 = jnp.bfloat16
    freq = jnp.asarray(frequency_row())
    spec = functools.partial(pl.BlockSpec, memory_space=VMEM)
    smem = pl.BlockSpec(memory_space=SMEM)
    anywhere = pl.BlockSpec(memory_space=pl.ANY)

    packed = pl.pallas_call(
        functools.partial(pack_queries, n_sub, group_size),
        out_shape=[jax.ShapeDtypeStruct((width, HD), bf16)] * n_req + [jax.ShapeDtypeStruct((kv_local, rows, HD), bf16)],
        in_specs=[spec()] * 4,
        out_specs=[spec()] * (n_req + 1),
        scratch_shapes=[pltpu.VMEM((rows, HD), jnp.float32)] * 2,
        name="pack_queries",
    )(freq, row_positions, queries, fresh_rows)
    sent_queries, own_key = packed[:n_req], packed[n_req]

    level_rows = max(HD, n_req * sub_heads)
    own = pl.pallas_call(
        functools.partial(own_scores, n_sub, group_size),
        out_shape=jax.ShapeDtypeStruct((rows, level_rows), jnp.float32),
        in_specs=[spec()] * (1 + n_req),
        out_specs=spec(),
        name="own_scores",
    )(own_key, *sent_queries)
    lengths_after = lax.optimization_barrier((lengths, sent_queries[0]))[0]

    packed_kv = pl.pallas_call(
        functools.partial(pack_kv, n_sub),
        grid=(blk_dev,),
        out_shape=[jax.ShapeDtypeStruct((blk_dev, block_len + TAG, 2 * HD), bf16)] * kv_heads,
        in_specs=[smem, smem, pl.BlockSpec((1, HD), lambda i: (0, 0)), pl.BlockSpec((1, block_len, full_width), lambda i: (i, 0, 0))],
        out_specs=[pl.BlockSpec((1, block_len + TAG, 2 * HD), lambda i: (i, 0, 0))] * kv_heads,
        name="pack_kv",
    )(block_order, lengths_after, freq, kv_store)

    to_compute = []
    for step in range(n_req):
        pairs = []
        for request in range(n_req):
            for h in range(n_sub):
                head = kv_local * h + ((step % kv_local) ^ (request % kv_local))
                sub = (step // kv_local) ^ (request // kv_local)
                pairs.append((request * n_sub + h, head * n_sub + sub))
        to_compute.append(pairs)
    held_queries = [moved(x, pairs) for x, pairs in zip(sent_queries, to_compute)]

    wide_rows = jnp.tile(row_positions, (1, sub_heads))[:, None, :]

    def after(x, *others):
        return lax.optimization_barrier((x, *others))[0] if others else x

    def at_head(mask, *others):
        pairs = [(d, ((d // n_sub) ^ mask) * n_sub + d % n_sub) for d in range(n_shard)]
        return packed_kv[0] if mask == 0 else moved(after(packed_kv[mask], *others), pairs)

    def from_sub(mask, back, *others):
        x = landed[mask]
        pairs = [(d, (d // n_sub) * n_sub + (d % n_sub + back) % n_sub) for d in range(n_shard)]
        return x if back == 0 else moved(after(x, *others), pairs)

    half = kv_heads // 2
    groups = [[0], list(range(1, half)), [half, half + 1]] + [[mask] for mask in range(half + 2, kv_heads)]
    landed = {mask: at_head(mask) for mask in range(half + 2)}
    landed[half + 2] = at_head(half + 2, *held_queries)
    state_shapes = [
        jax.ShapeDtypeStruct((n_req, HD + 8, width), jnp.float32),
        jax.ShapeDtypeStruct((n_req, 1, width), jnp.float32),
    ]
    part_shapes = [jax.ShapeDtypeStruct((width + STATS, HD), bf16)] * n_req
    state, older = [], []
    for index, masks in enumerate(groups):
        if index == 2:
            for mask in range(half + 3, kv_heads):
                if mask not in landed:
                    landed[mask] = at_head(mask, *state[-1:], landed[masks[0]])
        gate = state if index <= 2 else older
        arrived = [from_sub(mask, back, *gate[-1:]) for mask in masks for back in range(n_sub)]
        buffers = [(mask, back) for mask in masks for back in range(n_sub)]
        first, last = index == 0, index == len(groups) - 1
        blocks = len(buffers) * blk_dev
        results = pl.pallas_call(
            functools.partial(attend, n_sub, len(buffers), first, last, blk_dev),
            out_shape=part_shapes if last else state_shapes,
            in_specs=[smem, spec()] + [anywhere] * (n_req + len(buffers)) + [spec()] * len(state),
            out_specs=[spec()] * (n_req if last else 2),
            scratch_shapes=([pltpu.VMEM(s.shape, s.dtype) for s in state_shapes] if last else [])
            + [
                pltpu.VMEM((n_req, width, HD), bf16),
                pltpu.VMEM((blocks, block_len + TAG, 2 * HD), bf16),
                pltpu.SMEM((blocks,), jnp.int32),
                pltpu.SemaphoreType.DMA((n_req,)),
                pltpu.SemaphoreType.DMA((len(buffers),)),
            ],
        )(lengths, wide_rows, *held_queries, *arrived, *state)
        older, state = state, list(results)
    returned = []
    for part, pairs in zip(state, to_compute):
        returned.append(lax.ppermute(part, "shard", [(b, a) for a, b in pairs]))

    return pl.pallas_call(
        functools.partial(merge_own, n_sub, group_size),
        out_shape=jax.ShapeDtypeStruct((rows, kv_local * group_size * HD), bf16),
        in_specs=[spec()] * (2 + n_req),
        out_specs=spec(),
        scratch_shapes=[pltpu.VMEM((level_rows, rows), jnp.float32)],
        name="merge_own",
    )(own, fresh_rows, *returned)


def solution(mesh):
    in_specs = (
        P(("groups", "shard"), None, None),
        P(("groups", "shard")),
        P("groups"),
        P("groups", None),
        P("groups", "shard"),
        P("groups", "shard"),
    )
    return jax.shard_map(shards, mesh=mesh, in_specs=in_specs, out_specs=P("groups", "shard"), check_vma=False)
```

```python
import functools
import math

import jax
import jax.numpy as jnp
import numpy as np
from jax import lax
from jax.experimental import pallas as pl
from jax.experimental.pallas import tpu as pltpu
from jax.sharding import PartitionSpec as P


HD = 128
ROPE_BASE = 500000.0
TOP_START = -1e30
MASKED = -3e30
STATS = 16
TAG = 8
NOWHERE = 1 << 28
GRANT = 24 << 20


def tiles_of(width):
    return 2 if width % (4 * HD) == 0 else 1


def chunks_of(sub_heads, rows):
    tiles = tiles_of(sub_heads * rows)
    size = rows // tiles
    for tile in range(tiles):
        for head in range(sub_heads):
            start = (tile * sub_heads + head) * size
            yield head, slice(tile * size, (tile + 1) * size), slice(start, start + size)


VMEM = pltpu.MemorySpace.VMEM
SMEM = pltpu.MemorySpace.SMEM


def frequency_row():
    half = HD // 2
    steps = np.arange(half, dtype=np.float32)
    row = np.exp((-math.log(ROPE_BASE) * steps / half).astype(np.float32)).astype(np.float32)
    return np.concatenate([row, row])[None, :]


def signed(sine):
    lane = lax.broadcasted_iota(jnp.int32, sine.shape, len(sine.shape) - 1)
    return jnp.where(lane < HD // 2, -sine, sine)


def turn(vectors, cosine, sine):
    wide = vectors.astype(jnp.float32)
    return (wide * cosine + pltpu.roll(wide, HD // 2, 1) * sine).astype(jnp.bfloat16)


def find_block(block_id, lengths_ref):
    start = jnp.int32(0)
    request = jnp.int32(0)
    position = jnp.int32(0)
    for q in range(lengths_ref.shape[0]):
        end = start + lengths_ref[q]
        inside = (block_id >= start) & (block_id < end)
        request = jnp.where(inside, q, request)
        position = jnp.where(inside, block_id - start, position)
        start = end
    return request, position


def pack_kv(n_sub, order_ref, lengths_ref, freq_ref, kv_ref, *out_refs):
    heads = len(out_refs)
    my_head = lax.axis_index("shard") // n_sub
    block_len = kv_ref.shape[1]
    block_id = order_ref[pl.program_id(0)]
    request, position = find_block(block_id, lengths_ref)
    left = lax.broadcasted_iota(jnp.int32, (TAG, 2 * HD), 1) < HD
    tag = jnp.where(left, request, position).astype(jnp.float32).astype(jnp.bfloat16)
    angle = (position * block_len).astype(jnp.float32) * freq_ref[...]
    cosine, sine = jnp.cos(angle), signed(jnp.sin(angle))
    for mask in range(heads):
        column = pl.multiple_of((my_head ^ mask) * (2 * HD), 2 * HD)
        out_refs[mask][0, :block_len, :HD] = turn(kv_ref[0, :, pl.ds(column, HD)], cosine, sine)
        out_refs[mask][0, :block_len, HD:] = kv_ref[0, :, pl.ds(column + HD, HD)]
        out_refs[mask][0, block_len:, :] = tag


def pack_queries(n_sub, group_size, freq_ref, rows_ref, queries_ref, fresh_ref, *refs):
    out_refs, key_ref, wide_ref, cos_ref, sin_ref = refs[:-4], refs[-4], refs[-3], refs[-2], refs[-1]
    request = lax.axis_index("shard") // n_sub
    rows = queries_ref.shape[0]
    kv_local = fresh_ref.shape[1] // (2 * HD)
    sub_heads = group_size // n_sub
    position = rows_ref[pl.ds(request, 1), :].astype(jnp.float32)
    angle = jnp.transpose(jnp.broadcast_to(position, (HD, rows))) * freq_ref[...]
    cos_ref[...] = jnp.cos(angle)
    sin_ref[...] = signed(jnp.sin(angle))
    for step, out_ref in enumerate(out_refs):
        kv_id = (step % kv_local) ^ (request % kv_local)
        sub = (step // kv_local) ^ (request // kv_local)
        for head, row_part, flat in chunks_of(sub_heads, rows):
            column = pl.multiple_of((kv_id * group_size + sub * sub_heads + head) * HD, HD)
            out_ref[flat, :] = turn(queries_ref[row_part, pl.ds(column, HD)], cos_ref[row_part, :], sin_ref[row_part, :])
    for kv_id in range(kv_local):
        key_ref[kv_id] = turn(fresh_ref[:, 2 * kv_id * HD : (2 * kv_id + 1) * HD], cos_ref[...], sin_ref[...])
    tiles = tiles_of(sub_heads * rows)
    size = rows // tiles
    n_req = rows_ref.shape[0]
    for tile in range(tiles):
        wide = jnp.concatenate([rows_ref[:, tile * size : (tile + 1) * size]] * sub_heads, axis=1)
        for r in range(n_req):
            wide_ref[tile * n_req + r] = wide[r : r + 1]


def attend(n_sub, n_buf, first, last, blk_dev, rows_smem, wide_ref, *refs):
    n_req = rows_smem.shape[0]
    rows = rows_smem.shape[1]
    if first:
        query_refs, refs = refs[:n_req], refs[n_req:]
    kv_refs, refs = refs[:n_buf], refs[n_buf:]
    if not first:
        refs = refs[3:]
    if last:
        out_refs, refs = refs[:n_req], refs[n_req:]
    acc_ref, top_ref, query_buf, kv_buf, score_a, score_b, best_a, best_b, item_ref, query_sem, kv_sem = refs
    tiles, half = query_buf.shape[1:3]
    query_copies = [
        pltpu.make_async_copy(ref.at[pl.ds(tile * half, half)], query_buf.at[i, tile], query_sem.at[i, tile])
        for i, ref in enumerate(query_refs)
        for tile in range(tiles)
    ] if first else []
    kv_copies = [
        pltpu.make_async_copy(ref, kv_buf.at[pl.ds(i * blk_dev, blk_dev)], kv_sem.at[i]) for i, ref in enumerate(kv_refs)
    ]
    for copy in kv_copies + query_copies:
        copy.start()
    me = lax.axis_index("shard")
    my_head, my_sub = me // n_sub, me % n_sub
    kv_local = n_req // n_sub
    mixed = my_sub * kv_local + my_head % kv_local
    block_len = kv_buf.shape[1] - TAG
    if first:
        acc_ref[...] = jnp.zeros_like(acc_ref)
        top_ref[...] = jnp.full_like(top_ref, TOP_START)
    for copy in kv_copies:
        copy.wait()
    count = jnp.int32(0)
    for i in range(n_buf * blk_dev):
        tag = kv_buf[i, block_len:, :].astype(jnp.float32)
        request = jnp.max(tag[:, :HD]).astype(jnp.int32)
        offset = jnp.max(tag[:, HD:]).astype(jnp.int32) * block_len
        for tile in reversed(range(tiles)):
            item_ref[0, count] = i
            item_ref[1, count] = request
            item_ref[2, count] = tile
            item_ref[3, count] = offset
            used = rows_smem[request, (tile + 1) * (rows // tiles) - 1] > offset
            count = count + jnp.where(used, 1, 0)
    for pad in range(2):
        item_ref[0, count + pad] = 0
        item_ref[1, count + pad] = 0
        item_ref[2, count + pad] = 0
        item_ref[3, count + pad] = NOWHERE
    for copy in query_copies:
        copy.wait()
    scale = math.log2(math.e) / math.sqrt(HD)
    token = lax.broadcasted_iota(jnp.int32, (block_len, half), 0)

    def score(item, score_ref, best_ref):
        i, request, tile = item_ref[0, item], item_ref[1, item], item_ref[2, item]
        scores = lax.dot_general(
            kv_buf[i, :block_len, :HD],
            query_buf[request ^ mixed, tile],
            (((1,), (1,)), ((), ())),
            preferred_element_type=jnp.float32,
        )
        limit = wide_ref[tile * n_req + request] - item_ref[3, item]
        scores = jnp.where(token < limit, scores * scale, MASKED)
        score_ref[...] = scores
        best_ref[...] = jnp.max(scores, axis=0, keepdims=True)

    def add(item, score_ref, best_ref):
        i = item_ref[0, item]
        place = item_ref[2, item] * n_req + item_ref[1, item]
        old_top = top_ref[place]
        new_top = jnp.maximum(old_top, best_ref[...])
        factor = jnp.exp2(old_top - new_top)
        weights = jnp.exp2(score_ref[...] - new_top).astype(jnp.bfloat16)
        values = jnp.concatenate(
            [jnp.transpose(kv_buf[i, :block_len, HD:]), jnp.ones((STATS, block_len), jnp.bfloat16)], axis=0
        )
        summed = jnp.dot(values, weights, preferred_element_type=jnp.float32)
        acc_ref[place] = acc_ref[place] * factor + summed[: HD + 8]
        top_ref[place] = new_top

    score(0, score_a, best_a)

    def two_items(j, carried):
        score(2 * j + 1, score_b, best_b)
        add(2 * j, score_a, best_a)
        score(2 * j + 2, score_a, best_a)
        add(2 * j + 1, score_b, best_b)
        return carried

    lax.fori_loop(0, (count + 1) // 2, two_items, 0)

    if last:
        for step, out_ref in enumerate(out_refs):
            request = step ^ mixed
            levels = []
            for tile in range(tiles):
                place = tile * n_req + request
                total = acc_ref[place, HD : HD + 1]
                some = total > 0.0
                safe = jnp.where(some, total, 1.0)
                result = acc_ref[place, :HD] * (1.0 / safe)
                out_ref[tile * half : (tile + 1) * half, :] = jnp.transpose(result).astype(jnp.bfloat16)
                level = jnp.where(some, top_ref[place] + jnp.log2(safe), TOP_START)
                levels += [level[:, at * HD : (at + 1) * HD] for at in range(half // HD)]
            level = jnp.concatenate(levels, axis=0)
            high = level.astype(jnp.bfloat16)
            rest = level - high.astype(jnp.float32)
            middle = rest.astype(jnp.bfloat16)
            low = (rest - middle.astype(jnp.float32)).astype(jnp.bfloat16)
            pieces = [high, middle, low, jnp.zeros((STATS - 3 * len(levels), HD), jnp.bfloat16)]
            out_ref[tiles * half :, :] = jnp.concatenate(pieces, axis=0)


def own_scores(n_sub, group_size, key_ref, *refs):
    query_refs, own_ref = refs[:-1], refs[-1]
    request = lax.axis_index("shard") // n_sub
    kv_local, rows = key_ref.shape[:2]
    sub_heads = group_size // n_sub
    lines = sub_heads * rows // HD
    scale = math.log2(math.e) / math.sqrt(HD)
    own_ref[...] = jnp.zeros_like(own_ref)
    for step, query_ref in enumerate(query_refs):
        own_key = key_ref[(step % kv_local) ^ (request % kv_local)].astype(jnp.float32)
        for head, row_part, flat in chunks_of(sub_heads, rows):
            query = query_ref[flat, :].astype(jnp.float32)
            line, at = step * lines + flat.start // HD, flat.start % HD
            own = jnp.sum(query * own_key[row_part, :], axis=1, keepdims=True) * scale
            own_ref[at : at + own.shape[0], line : line + 1] = own


def merge_own(n_sub, group_size, own_ref, fresh_ref, *refs):
    part_refs, out_ref, level_ref = refs[:-2], refs[-2], refs[-1]
    request = lax.axis_index("shard") // n_sub
    rows = out_ref.shape[0]
    kv_local = fresh_ref.shape[1] // (2 * HD)
    sub_heads = group_size // n_sub
    width = sub_heads * rows
    lines = width // HD
    level_ref[...] = jnp.zeros_like(level_ref)
    for step, part_ref in enumerate(part_refs):
        stats = part_ref[width:, :].astype(jnp.float32)
        level_ref[step * lines : (step + 1) * lines] = stats[:lines] + stats[lines : 2 * lines] + stats[2 * lines : 3 * lines]
    level = jnp.transpose(level_ref[...])
    own = own_ref[...]
    top = jnp.maximum(own, level)
    own_share = jnp.exp2(own - top)
    share = jnp.exp2(level - top)
    norm = 1.0 / (own_share + share)
    own_share, share = own_share * norm, share * norm
    for step, part_ref in enumerate(part_refs):
        kv_id = (step % kv_local) ^ (request % kv_local)
        sub = (step // kv_local) ^ (request // kv_local)
        value_column = pl.multiple_of((2 * kv_id + 1) * HD, HD)
        own_value = fresh_ref[:, pl.ds(value_column, HD)].astype(jnp.float32)
        for head, row_part, flat in chunks_of(sub_heads, rows):
            line, at = step * lines + flat.start // HD, flat.start % HD
            size = flat.stop - flat.start
            part = part_ref[flat, :].astype(jnp.float32)
            column = pl.multiple_of((kv_id * group_size + sub * sub_heads + head) * HD, HD)
            out_ref[row_part, pl.ds(column, HD)] = (
                part * share[at : at + size, line : line + 1]
                + own_value[row_part, :] * own_share[at : at + size, line : line + 1]
            ).astype(jnp.bfloat16)


def moved(x, pairs):
    return lax.ppermute(x, "shard", pairs)


def shards(kv_store, block_order, lengths, row_positions, queries, fresh_rows):
    n_shard = lax.axis_size("shard")
    n_req, rows = row_positions.shape
    n_sub = n_shard // n_req
    blk_dev, block_len, full_width = kv_store.shape
    kv_heads = full_width // (2 * HD)
    kv_local = kv_heads // n_sub
    group_size = queries.shape[1] // (kv_local * HD)
    sub_heads = group_size // n_sub
    width = sub_heads * rows
    tiles = tiles_of(width)
    half_width = width // tiles
    bf16 = jnp.bfloat16
    freq = jnp.asarray(frequency_row())
    spec = functools.partial(pl.BlockSpec, memory_space=VMEM)
    smem = pl.BlockSpec(memory_space=SMEM)
    anywhere = pl.BlockSpec(memory_space=pl.ANY)

    packed = pl.pallas_call(
        functools.partial(pack_queries, n_sub, group_size),
        out_shape=[jax.ShapeDtypeStruct((width, HD), bf16)] * n_req + [
            jax.ShapeDtypeStruct((kv_local, rows, HD), bf16),
            jax.ShapeDtypeStruct((n_req * tiles, 1, width // tiles), jnp.int32),
        ],
        in_specs=[spec()] * 4,
        out_specs=[spec()] * (n_req + 2),
        scratch_shapes=[pltpu.VMEM((rows, HD), jnp.float32)] * 2,
        compiler_params=pltpu.CompilerParams(vmem_limit_bytes=GRANT),
        name="pack_queries",
    )(freq, row_positions, queries, fresh_rows)
    sent_queries, own_key, wide_rows = packed[:n_req], packed[n_req], packed[n_req + 1]

    level_rows = max(HD, n_req * width // HD)
    own = pl.pallas_call(
        functools.partial(own_scores, n_sub, group_size),
        out_shape=jax.ShapeDtypeStruct((rows, level_rows), jnp.float32),
        in_specs=[spec()] * (1 + n_req),
        out_specs=spec(),
        compiler_params=pltpu.CompilerParams(vmem_limit_bytes=GRANT),
        name="own_scores",
    )(own_key, *sent_queries)
    lengths_after = lax.optimization_barrier((lengths, sent_queries[0]))[0]

    packed_kv = pl.pallas_call(
        functools.partial(pack_kv, n_sub),
        grid=(blk_dev,),
        out_shape=[jax.ShapeDtypeStruct((blk_dev, block_len + TAG, 2 * HD), bf16)] * kv_heads,
        in_specs=[smem, smem, pl.BlockSpec((1, HD), lambda i: (0, 0)), pl.BlockSpec((1, block_len, full_width), lambda i: (i, 0, 0))],
        out_specs=[pl.BlockSpec((1, block_len + TAG, 2 * HD), lambda i: (i, 0, 0))] * kv_heads,
        compiler_params=pltpu.CompilerParams(vmem_limit_bytes=GRANT),
        name="pack_kv",
    )(block_order, lengths_after, freq, kv_store)

    to_compute = []
    for step in range(n_req):
        pairs = []
        for request in range(n_req):
            for h in range(n_sub):
                head = kv_local * h + ((step % kv_local) ^ (request % kv_local))
                sub = (step // kv_local) ^ (request // kv_local)
                pairs.append((request * n_sub + h, head * n_sub + sub))
        to_compute.append(pairs)
    held_queries = [moved(x, pairs) for x, pairs in zip(sent_queries, to_compute)]


    def after(x, *others):
        return lax.optimization_barrier((x, *others))[0] if others else x

    def at_head(mask, *others):
        pairs = [(d, ((d // n_sub) ^ mask) * n_sub + d % n_sub) for d in range(n_shard)]
        return packed_kv[0] if mask == 0 else moved(after(packed_kv[mask], *others), pairs)

    def from_sub(mask, back, *others):
        x = landed[mask]
        pairs = [(d, (d // n_sub) * n_sub + (d % n_sub + back) % n_sub) for d in range(n_shard)]
        return x if back == 0 else moved(after(x, *others), pairs)

    half = kv_heads // 2
    groups = [[0], list(range(1, half)), [half, half + 1]] + [[mask] for mask in range(half + 2, kv_heads)]
    landed = {mask: at_head(mask) for mask in range(half + 2)}
    landed[half + 2] = at_head(half + 2, *held_queries)
    state_shapes = [
        pltpu.VMEM((n_req * tiles, HD + 8, half_width), jnp.float32),
        pltpu.VMEM((n_req * tiles, 1, half_width), jnp.float32),
        pltpu.VMEM((n_req, tiles, half_width, HD), bf16),
    ]
    part_shapes = [jax.ShapeDtypeStruct((width + STATS, HD), bf16)] * n_req
    state, older = [], []
    for index, masks in enumerate(groups):
        if index == 1:
            for mask in range(half + 3, kv_heads):
                if mask not in landed:
                    landed[mask] = at_head(mask, landed[half - 1])
        gate = state if index <= 2 else older
        arrived = [from_sub(mask, back, *gate[-1:]) for mask in masks for back in range(n_sub)]
        buffers = [(mask, back) for mask in masks for back in range(n_sub)]
        first, last = index == 0, index == len(groups) - 1
        blocks = len(buffers) * blk_dev
        inputs = [*(held_queries if first else []), *arrived]
        results = pl.pallas_call(
            functools.partial(attend, n_sub, len(buffers), first, last, blk_dev),
            out_shape=(part_shapes if last else []) + state_shapes,
            in_specs=[smem, spec()] + [anywhere] * len(inputs) + [spec()] * len(state),
            out_specs=[spec()] * ((n_req if last else 0) + 3),
            input_output_aliases={2 + len(inputs) + k: (n_req if last else 0) + k for k in range(len(state))},
            scratch_shapes=[
                pltpu.VMEM((blocks, block_len + TAG, 2 * HD), bf16),
                pltpu.VMEM((block_len, half_width), jnp.float32),
                pltpu.VMEM((block_len, half_width), jnp.float32),
                pltpu.VMEM((1, half_width), jnp.float32),
                pltpu.VMEM((1, half_width), jnp.float32),
                pltpu.SMEM((4, blocks * tiles + 2), jnp.int32),
                pltpu.SemaphoreType.DMA((n_req, tiles)),
                pltpu.SemaphoreType.DMA((len(buffers),)),
            ],
            compiler_params=pltpu.CompilerParams(vmem_limit_bytes=GRANT),
        )(row_positions, wide_rows, *inputs, *state)
        older, state = state, list(results)
    returned = []
    for part, pairs in zip(state, to_compute):
        returned.append(lax.ppermute(part, "shard", [(b, a) for a, b in pairs]))

    return pl.pallas_call(
        functools.partial(merge_own, n_sub, group_size),
        out_shape=jax.ShapeDtypeStruct((rows, kv_local * group_size * HD), bf16),
        in_specs=[spec()] * (2 + n_req),
        out_specs=spec(),
        scratch_shapes=[pltpu.VMEM((level_rows, rows), jnp.float32)],
        compiler_params=pltpu.CompilerParams(vmem_limit_bytes=GRANT),
        name="merge_own",
    )(own, fresh_rows, *returned)


def solution(mesh):
    in_specs = (
        P(("groups", "shard"), None, None),
        P(("groups", "shard")),
        P("groups"),
        P("groups", None),
        P("groups", "shard"),
        P("groups", "shard"),
    )
    return jax.shard_map(shards, mesh=mesh, in_specs=in_specs, out_specs=P("groups", "shard"), check_vma=False)
```

```python
import functools
import math

import jax
import jax.numpy as jnp
from jax import lax
from jax.experimental import pallas as pl
from jax.experimental.pallas import tpu as pltpu
from jax.sharding import PartitionSpec as P


HD = 128
ROPE_BASE = 500000.0
TOP_START = -1e30
MASKED = -3e30
STATS = 16
TAG = 8
NOWHERE = 1 << 28
GRANT = 24 << 20


def tiles_of(width):
    return 2 if width % (4 * HD) == 0 else 1


def chunks_of(sub_heads, rows):
    tiles = tiles_of(sub_heads * rows)
    size = rows // tiles
    for tile in range(tiles):
        for head in range(sub_heads):
            start = (tile * sub_heads + head) * size
            yield head, slice(tile * size, (tile + 1) * size), slice(start, start + size)


VMEM = pltpu.MemorySpace.VMEM
SMEM = pltpu.MemorySpace.SMEM


def frequencies():
    half = HD // 2
    steps = lax.broadcasted_iota(jnp.int32, (1, HD), 1) % half
    return jnp.exp(-math.log(ROPE_BASE) * steps.astype(jnp.float32) / half)


def signed(sine):
    lane = lax.broadcasted_iota(jnp.int32, sine.shape, len(sine.shape) - 1)
    return jnp.where(lane < HD // 2, -sine, sine)


def turn(vectors, cosine, sine):
    wide = vectors.astype(jnp.float32)
    return (wide * cosine + pltpu.roll(wide, HD // 2, 1) * sine).astype(jnp.bfloat16)


def find_block(block_id, lengths_ref):
    start = jnp.int32(0)
    request = jnp.int32(0)
    position = jnp.int32(0)
    for q in range(lengths_ref.shape[0]):
        end = start + lengths_ref[q]
        inside = (block_id >= start) & (block_id < end)
        request = jnp.where(inside, q, request)
        position = jnp.where(inside, block_id - start, position)
        start = end
    return request, position


def pack_kv(n_sub, order_ref, lengths_ref, kv_ref, *refs):
    out_refs, buf, sem = refs[:-2], refs[-2], refs[-1]
    heads = len(out_refs)
    slots = buf.shape[0]
    copies = [pltpu.make_async_copy(kv_ref.at[slot], buf.at[slot], sem.at[slot]) for slot in range(slots)]
    for copy in copies:
        copy.start()
    my_head = lax.axis_index("shard") // n_sub
    block_len = buf.shape[1]
    left = lax.broadcasted_iota(jnp.int32, (TAG, 2 * HD), 1) < HD
    for slot in range(slots):
        request, position = find_block(order_ref[slot], lengths_ref)
        tag = jnp.where(left, request, position).astype(jnp.float32).astype(jnp.bfloat16)
        angle = (position * block_len).astype(jnp.float32) * frequencies()
        cosine, sine = jnp.cos(angle), signed(jnp.sin(angle))
        copies[slot].wait()
        for mask in range(heads):
            column = pl.multiple_of((my_head ^ mask) * (2 * HD), 2 * HD)
            out_refs[mask][slot, :block_len, :HD] = turn(buf[slot, :, pl.ds(column, HD)], cosine, sine)
            out_refs[mask][slot, :block_len, HD:] = buf[slot, :, pl.ds(column + HD, HD)]
            out_refs[mask][slot, block_len:, :] = tag


def row_turns(row):
    angle = jnp.transpose(jnp.broadcast_to(row.astype(jnp.float32), (HD, row.shape[1]))) * frequencies()
    return jnp.cos(angle), signed(jnp.sin(angle))


def pack_queries(n_sub, group_size, rows_ref, queries_ref, *refs):
    out_refs, (cos_ref, sin_ref, rows_buf, buf, sem) = refs[:-5], refs[-5:]
    request = lax.axis_index("shard") // n_sub
    kv_local = buf.shape[0]
    rows = buf.shape[1]
    span = group_size * HD
    rows_copy = pltpu.make_async_copy(rows_ref, rows_buf, sem.at[kv_local])
    rows_copy.start()
    copies = [
        pltpu.make_async_copy(queries_ref.at[:, pl.ds(kv_id * span, span)], buf.at[kv_id], sem.at[kv_id])
        for kv_id in range(kv_local)
    ]
    for copy in copies:
        copy.start()
    sub_heads = group_size // n_sub
    rows_copy.wait()
    cos_ref[...], sin_ref[...] = row_turns(rows_buf[pl.ds(request, 1), :])
    for copy in copies:
        copy.wait()
    for step, out_ref in enumerate(out_refs):
        kv_id = (step % kv_local) ^ (request % kv_local)
        sub = (step // kv_local) ^ (request // kv_local)
        for head, row_part, flat in chunks_of(sub_heads, rows):
            column = pl.multiple_of((sub * sub_heads + head) * HD, HD)
            out_ref[flat, :] = turn(buf[kv_id, row_part, pl.ds(column, HD)], cos_ref[row_part, :], sin_ref[row_part, :])


def attend(n_sub, n_buf, first, last, blk_dev, rows_smem, wide_ref, *refs):
    n_req = rows_smem.shape[0]
    rows = rows_smem.shape[1]
    if first:
        query_refs, refs = refs[:n_req], refs[n_req:]
    kv_refs, refs = refs[:n_buf], refs[n_buf:]
    if not first:
        refs = refs[3:]
    if last:
        out_refs, refs = refs[:n_req], refs[n_req:]
    acc_ref, top_ref, query_buf, kv_buf, score_a, score_b, best_a, best_b, item_ref, query_sem, kv_sem = refs
    tiles, half = query_buf.shape[1:3]
    query_copies = [
        pltpu.make_async_copy(ref.at[pl.ds(tile * half, half)], query_buf.at[i, tile], query_sem.at[i, tile])
        for i, ref in enumerate(query_refs)
        for tile in range(tiles)
    ] if first else []
    kv_copies = [
        pltpu.make_async_copy(ref, kv_buf.at[pl.ds(i * blk_dev, blk_dev)], kv_sem.at[i]) for i, ref in enumerate(kv_refs)
    ]
    for copy in kv_copies + query_copies:
        copy.start()
    me = lax.axis_index("shard")
    my_head, my_sub = me // n_sub, me % n_sub
    kv_local = n_req // n_sub
    mixed = my_sub * kv_local + my_head % kv_local
    block_len = kv_buf.shape[1] - TAG
    if first:
        acc_ref[...] = jnp.zeros_like(acc_ref)
        top_ref[...] = jnp.full_like(top_ref, TOP_START)
    for copy in kv_copies:
        copy.wait()
    count = jnp.int32(0)
    for i in range(n_buf * blk_dev):
        tag = kv_buf[i, block_len:, :].astype(jnp.float32)
        request = jnp.max(tag[:, :HD]).astype(jnp.int32)
        offset = jnp.max(tag[:, HD:]).astype(jnp.int32) * block_len
        for tile in reversed(range(tiles)):
            item_ref[0, count] = i
            item_ref[1, count] = request
            item_ref[2, count] = tile
            item_ref[3, count] = offset
            used = rows_smem[request, (tile + 1) * (rows // tiles) - 1] > offset
            count = count + jnp.where(used, 1, 0)
    for pad in range(2):
        item_ref[0, count + pad] = 0
        item_ref[1, count + pad] = 0
        item_ref[2, count + pad] = 0
        item_ref[3, count + pad] = NOWHERE
    for copy in query_copies:
        copy.wait()
    scale = math.log2(math.e) / math.sqrt(HD)
    token = lax.broadcasted_iota(jnp.int32, (block_len, half), 0)

    def score(item, score_ref, best_ref):
        i, request, tile = item_ref[0, item], item_ref[1, item], item_ref[2, item]
        scores = lax.dot_general(
            kv_buf[i, :block_len, :HD],
            query_buf[request ^ mixed, tile],
            (((1,), (1,)), ((), ())),
            preferred_element_type=jnp.float32,
        )
        limit = wide_ref[tile * n_req + request] - item_ref[3, item]
        scores = jnp.where(token < limit, scores * scale, MASKED)
        score_ref[...] = scores
        best_ref[...] = jnp.max(scores, axis=0, keepdims=True)

    def add(item, score_ref, best_ref):
        i = item_ref[0, item]
        place = item_ref[2, item] * n_req + item_ref[1, item]
        old_top = top_ref[place]
        new_top = jnp.maximum(old_top, best_ref[...])
        factor = jnp.exp2(old_top - new_top)
        weights = jnp.exp2(score_ref[...] - new_top).astype(jnp.bfloat16)
        values = jnp.concatenate(
            [jnp.transpose(kv_buf[i, :block_len, HD:]), jnp.ones((STATS, block_len), jnp.bfloat16)], axis=0
        )
        summed = jnp.dot(values, weights, preferred_element_type=jnp.float32)
        acc_ref[place] = acc_ref[place] * factor + summed[: HD + 8]
        top_ref[place] = new_top

    score(0, score_a, best_a)

    def two_items(j, carried):
        score(2 * j + 1, score_b, best_b)
        add(2 * j, score_a, best_a)
        score(2 * j + 2, score_a, best_a)
        add(2 * j + 1, score_b, best_b)
        return carried

    lax.fori_loop(0, (count + 1) // 2, two_items, 0)

    if last:
        for step, out_ref in enumerate(out_refs):
            request = step ^ mixed
            levels = []
            for tile in range(tiles):
                place = tile * n_req + request
                total = acc_ref[place, HD : HD + 1]
                some = total > 0.0
                safe = jnp.where(some, total, 1.0)
                result = acc_ref[place, :HD] * (1.0 / safe)
                out_ref[tile * half : (tile + 1) * half, :] = jnp.transpose(result).astype(jnp.bfloat16)
                level = jnp.where(some, top_ref[place] + jnp.log2(safe), TOP_START)
                levels += [level[:, at * HD : (at + 1) * HD] for at in range(half // HD)]
            level = jnp.concatenate(levels, axis=0)
            high = level.astype(jnp.bfloat16)
            rest = level - high.astype(jnp.float32)
            middle = rest.astype(jnp.bfloat16)
            low = (rest - middle.astype(jnp.float32)).astype(jnp.bfloat16)
            pieces = [high, middle, low, jnp.zeros((STATS - 3 * len(levels), HD), jnp.bfloat16)]
            out_ref[tiles * half :, :] = jnp.concatenate(pieces, axis=0)


def own_scores(n_sub, group_size, rows_ref, fresh_ref, *refs):
    query_refs, own_ref, wide_ref = refs[:-2], refs[-2], refs[-1]
    request = lax.axis_index("shard") // n_sub
    n_req, rows = rows_ref.shape
    kv_local = fresh_ref.shape[1] // (2 * HD)
    sub_heads = group_size // n_sub
    lines = sub_heads * rows // HD
    scale = math.log2(math.e) / math.sqrt(HD)
    own_ref[...] = jnp.zeros_like(own_ref)
    cosine, sine = row_turns(rows_ref[pl.ds(request, 1), :])
    for step, query_ref in enumerate(query_refs):
        kv_id = (step % kv_local) ^ (request % kv_local)
        column = pl.multiple_of(2 * kv_id * HD, HD)
        own_key = turn(fresh_ref[:, pl.ds(column, HD)], cosine, sine).astype(jnp.float32)
        for head, row_part, flat in chunks_of(sub_heads, rows):
            query = query_ref[flat, :].astype(jnp.float32)
            line, at = step * lines + flat.start // HD, flat.start % HD
            own = jnp.sum(query * own_key[row_part, :], axis=1, keepdims=True) * scale
            own_ref[at : at + own.shape[0], line : line + 1] = own
    tiles = tiles_of(sub_heads * rows)
    size = rows // tiles
    for tile in range(tiles):
        wide = jnp.concatenate([rows_ref[:, tile * size : (tile + 1) * size]] * sub_heads, axis=1)
        for r in range(n_req):
            wide_ref[tile * n_req + r] = wide[r : r + 1]


def merge_own(n_sub, group_size, own_ref, fresh_ref, *refs):
    part_refs, out_ref, level_ref = refs[:-2], refs[-2], refs[-1]
    request = lax.axis_index("shard") // n_sub
    rows = out_ref.shape[0]
    kv_local = fresh_ref.shape[1] // (2 * HD)
    sub_heads = group_size // n_sub
    width = sub_heads * rows
    lines = width // HD
    level_ref[...] = jnp.zeros_like(level_ref)
    for step, part_ref in enumerate(part_refs):
        stats = part_ref[width:, :].astype(jnp.float32)
        level_ref[step * lines : (step + 1) * lines] = stats[:lines] + stats[lines : 2 * lines] + stats[2 * lines : 3 * lines]
    level = jnp.transpose(level_ref[...])
    own = own_ref[...]
    top = jnp.maximum(own, level)
    own_share = jnp.exp2(own - top)
    share = jnp.exp2(level - top)
    norm = 1.0 / (own_share + share)
    own_share, share = own_share * norm, share * norm
    for step, part_ref in enumerate(part_refs):
        kv_id = (step % kv_local) ^ (request % kv_local)
        sub = (step // kv_local) ^ (request // kv_local)
        value_column = pl.multiple_of((2 * kv_id + 1) * HD, HD)
        own_value = fresh_ref[:, pl.ds(value_column, HD)].astype(jnp.float32)
        for head, row_part, flat in chunks_of(sub_heads, rows):
            line, at = step * lines + flat.start // HD, flat.start % HD
            size = flat.stop - flat.start
            part = part_ref[flat, :].astype(jnp.float32)
            column = pl.multiple_of((kv_id * group_size + sub * sub_heads + head) * HD, HD)
            out_ref[row_part, pl.ds(column, HD)] = (
                part * share[at : at + size, line : line + 1]
                + own_value[row_part, :] * own_share[at : at + size, line : line + 1]
            ).astype(jnp.bfloat16)


def moved(x, pairs):
    return lax.ppermute(x, "shard", pairs)


def shards(kv_store, block_order, lengths, row_positions, queries, fresh_rows):
    n_shard = lax.axis_size("shard")
    n_req, rows = row_positions.shape
    n_sub = n_shard // n_req
    blk_dev, block_len, full_width = kv_store.shape
    kv_heads = full_width // (2 * HD)
    kv_local = kv_heads // n_sub
    group_size = queries.shape[1] // (kv_local * HD)
    sub_heads = group_size // n_sub
    width = sub_heads * rows
    tiles = tiles_of(width)
    half_width = width // tiles
    bf16 = jnp.bfloat16
    spec = functools.partial(pl.BlockSpec, memory_space=VMEM)
    smem = pl.BlockSpec(memory_space=SMEM)
    anywhere = pl.BlockSpec(memory_space=pl.ANY)

    grant = pltpu.CompilerParams(vmem_limit_bytes=GRANT)
    sent_queries = pl.pallas_call(
        functools.partial(pack_queries, n_sub, group_size),
        out_shape=[jax.ShapeDtypeStruct((width, HD), bf16)] * n_req,
        in_specs=[anywhere] * 2,
        out_specs=[spec()] * n_req,
        scratch_shapes=[
            pltpu.VMEM((rows, HD), jnp.float32),
            pltpu.VMEM((rows, HD), jnp.float32),
            pltpu.VMEM((n_req, rows), jnp.int32),
            pltpu.VMEM((kv_local, rows, group_size * HD), bf16),
            pltpu.SemaphoreType.DMA((kv_local + 1,)),
        ],
        compiler_params=grant,
        name="pack_queries",
    )(row_positions, queries)
    level_rows = max(HD, n_req * width // HD)
    own, wide_rows = pl.pallas_call(
        functools.partial(own_scores, n_sub, group_size),
        out_shape=[
            jax.ShapeDtypeStruct((rows, level_rows), jnp.float32),
            jax.ShapeDtypeStruct((n_req * tiles, 1, width // tiles), jnp.int32),
        ],
        in_specs=[spec()] * (2 + n_req),
        out_specs=[spec()] * 2,
        compiler_params=grant,
        name="own_scores",
    )(row_positions, fresh_rows, *sent_queries)
    lengths_after = lax.optimization_barrier((lengths, sent_queries[0]))[0]

    packed_kv = pl.pallas_call(
        functools.partial(pack_kv, n_sub),
        out_shape=[jax.ShapeDtypeStruct((blk_dev, block_len + TAG, 2 * HD), bf16)] * kv_heads,
        in_specs=[smem, smem, anywhere],
        out_specs=[spec()] * kv_heads,
        scratch_shapes=[pltpu.VMEM((blk_dev, block_len, full_width), bf16), pltpu.SemaphoreType.DMA((blk_dev,))],
        compiler_params=grant,
        name="pack_kv",
    )(block_order, lengths_after, kv_store)

    to_compute = []
    for step in range(n_req):
        pairs = []
        for request in range(n_req):
            for h in range(n_sub):
                head = kv_local * h + ((step % kv_local) ^ (request % kv_local))
                sub = (step // kv_local) ^ (request // kv_local)
                pairs.append((request * n_sub + h, head * n_sub + sub))
        to_compute.append(pairs)
    held_queries = [moved(x, pairs) for x, pairs in zip(sent_queries, to_compute)]


    def after(x, *others):
        return lax.optimization_barrier((x, *others))[0] if others else x

    def at_head(mask, *others):
        pairs = [(d, ((d // n_sub) ^ mask) * n_sub + d % n_sub) for d in range(n_shard)]
        return packed_kv[0] if mask == 0 else moved(after(packed_kv[mask], *others), pairs)

    def from_sub(mask, back, *others):
        x = landed[mask]
        pairs = [(d, (d // n_sub) * n_sub + (d % n_sub + back) % n_sub) for d in range(n_shard)]
        return x if back == 0 else moved(after(x, *others), pairs)

    half = kv_heads // 2
    groups = [[0], list(range(1, half)), [half, half + 1]] + [[mask] for mask in range(half + 2, kv_heads)]
    landed = {mask: at_head(mask) for mask in range(half + 2)}
    landed[half + 2] = at_head(half + 2, *held_queries)
    state_shapes = [
        pltpu.VMEM((n_req * tiles, HD + 8, half_width), jnp.float32),
        pltpu.VMEM((n_req * tiles, 1, half_width), jnp.float32),
        pltpu.VMEM((n_req, tiles, half_width, HD), bf16),
    ]
    part_shapes = [jax.ShapeDtypeStruct((width + STATS, HD), bf16)] * n_req
    state, older = [], []
    for index, masks in enumerate(groups):
        if index == 1:
            for mask in range(half + 3, kv_heads):
                if mask not in landed:
                    landed[mask] = at_head(mask, landed[half - 1])
        gate = state if index <= 2 else older
        arrived = [from_sub(mask, back, *gate[-1:]) for mask in masks for back in range(n_sub)]
        buffers = [(mask, back) for mask in masks for back in range(n_sub)]
        first, last = index == 0, index == len(groups) - 1
        blocks = len(buffers) * blk_dev
        inputs = [*(held_queries if first else []), *arrived]
        results = pl.pallas_call(
            functools.partial(attend, n_sub, len(buffers), first, last, blk_dev),
            out_shape=(part_shapes if last else []) + state_shapes,
            in_specs=[smem, spec()] + [anywhere] * len(inputs) + [spec()] * len(state),
            out_specs=[spec()] * ((n_req if last else 0) + 3),
            input_output_aliases={2 + len(inputs) + k: (n_req if last else 0) + k for k in range(len(state))},
            scratch_shapes=[
                pltpu.VMEM((blocks, block_len + TAG, 2 * HD), bf16),
                pltpu.VMEM((block_len, half_width), jnp.float32),
                pltpu.VMEM((block_len, half_width), jnp.float32),
                pltpu.VMEM((1, half_width), jnp.float32),
                pltpu.VMEM((1, half_width), jnp.float32),
                pltpu.SMEM((4, blocks * tiles + 2), jnp.int32),
                pltpu.SemaphoreType.DMA((n_req, tiles)),
                pltpu.SemaphoreType.DMA((len(buffers),)),
            ],
            compiler_params=grant,
        )(row_positions, wide_rows, *inputs, *state)
        older, state = state, list(results)
    returned = [moved(part, [(b, a) for a, b in pairs]) for part, pairs in zip(state, to_compute)]

    return pl.pallas_call(
        functools.partial(merge_own, n_sub, group_size),
        out_shape=jax.ShapeDtypeStruct((rows, kv_local * group_size * HD), bf16),
        in_specs=[spec()] * (2 + n_req),
        out_specs=spec(),
        scratch_shapes=[pltpu.VMEM((level_rows, rows), jnp.float32)],
        compiler_params=grant,
        name="merge_own",
    )(own, fresh_rows, *returned)


def solution(mesh):
    in_specs = (
        P(("groups", "shard"), None, None),
        P(("groups", "shard")),
        P("groups"),
        P("groups", None),
        P("groups", "shard"),
        P("groups", "shard"),
    )
    return jax.shard_map(shards, mesh=mesh, in_specs=in_specs, out_specs=P("groups", "shard"), check_vma=False)
```

```python
import functools
import math

import jax
import jax.numpy as jnp
from jax import lax
from jax.experimental import pallas as pl
from jax.experimental.pallas import tpu as pltpu
from jax.sharding import PartitionSpec as P


HD = 128
ROPE_BASE = 500000.0
TOP_START = -1e30
MASKED = -3e30
STATS = 16
TAG = 8
NOWHERE = 1 << 28
GRANT = 24 << 20


def tiles_of(width):
    return 2 if width % (4 * HD) == 0 else 1


def chunks_of(sub_heads, rows):
    tiles = tiles_of(sub_heads * rows)
    size = rows // tiles
    for tile in range(tiles):
        for head in range(sub_heads):
            start = (tile * sub_heads + head) * size
            yield head, slice(tile * size, (tile + 1) * size), slice(start, start + size)


VMEM = pltpu.MemorySpace.VMEM
SMEM = pltpu.MemorySpace.SMEM


def frequencies():
    half = HD // 2
    steps = lax.broadcasted_iota(jnp.int32, (1, HD), 1) % half
    return jnp.exp(-math.log(ROPE_BASE) * steps.astype(jnp.float32) / half)


def signed(sine):
    lane = lax.broadcasted_iota(jnp.int32, sine.shape, len(sine.shape) - 1)
    return jnp.where(lane < HD // 2, -sine, sine)


def turn(vectors, cosine, sine):
    wide = vectors.astype(jnp.float32)
    return (wide * cosine + pltpu.roll(wide, HD // 2, 1) * sine).astype(jnp.bfloat16)


def find_block(block_id, lengths_ref):
    start = jnp.int32(0)
    request = jnp.int32(0)
    position = jnp.int32(0)
    for q in range(lengths_ref.shape[0]):
        end = start + lengths_ref[q]
        inside = (block_id >= start) & (block_id < end)
        request = jnp.where(inside, q, request)
        position = jnp.where(inside, block_id - start, position)
        start = end
    return request, position


def pack_kv(n_sub, order_ref, lengths_ref, kv_ref, *refs):
    out_refs, buf, sem = refs[:-2], refs[-2], refs[-1]
    heads = len(out_refs)
    slots = buf.shape[0]
    copies = [pltpu.make_async_copy(kv_ref.at[slot], buf.at[slot], sem.at[slot]) for slot in range(slots)]
    for copy in copies:
        copy.start()
    my_head = lax.axis_index("shard") // n_sub
    block_len = buf.shape[1]
    left = lax.broadcasted_iota(jnp.int32, (TAG, 2 * HD), 1) < HD
    for slot in range(slots):
        request, position = find_block(order_ref[slot], lengths_ref)
        tag = jnp.where(left, request, position).astype(jnp.float32).astype(jnp.bfloat16)
        angle = (position * block_len).astype(jnp.float32) * frequencies()
        cosine, sine = jnp.cos(angle), signed(jnp.sin(angle))
        copies[slot].wait()
        for mask in range(heads):
            column = pl.multiple_of((my_head ^ mask) * (2 * HD), 2 * HD)
            out_refs[mask][slot, :block_len, :HD] = turn(buf[slot, :, pl.ds(column, HD)], cosine, sine)
            out_refs[mask][slot, :block_len, HD:] = buf[slot, :, pl.ds(column + HD, HD)]
            out_refs[mask][slot, block_len:, :] = tag


def row_turns(row):
    angle = jnp.transpose(jnp.broadcast_to(row.astype(jnp.float32), (HD, row.shape[1]))) * frequencies()
    return jnp.cos(angle), signed(jnp.sin(angle))


def pack_queries(n_sub, group_size, rows_ref, queries_ref, *refs):
    out_refs, (cos_ref, sin_ref, rows_buf, buf, sem) = refs[:-5], refs[-5:]
    request = lax.axis_index("shard") // n_sub
    kv_local = buf.shape[0]
    rows = buf.shape[1]
    span = group_size * HD
    rows_copy = pltpu.make_async_copy(rows_ref, rows_buf, sem.at[kv_local])
    rows_copy.start()
    copies = [
        pltpu.make_async_copy(queries_ref.at[:, pl.ds(kv_id * span, span)], buf.at[kv_id], sem.at[kv_id])
        for kv_id in range(kv_local)
    ]
    for copy in copies:
        copy.start()
    sub_heads = group_size // n_sub
    rows_copy.wait()
    cos_ref[...], sin_ref[...] = row_turns(rows_buf[pl.ds(request, 1), :])
    for copy in copies:
        copy.wait()
    for step, out_ref in enumerate(out_refs):
        kv_id = (step % kv_local) ^ (request % kv_local)
        sub = (step // kv_local) ^ (request // kv_local)
        for head, row_part, flat in chunks_of(sub_heads, rows):
            column = pl.multiple_of((sub * sub_heads + head) * HD, HD)
            out_ref[flat, :] = turn(buf[kv_id, row_part, pl.ds(column, HD)], cos_ref[row_part, :], sin_ref[row_part, :])


def attend(n_sub, n_buf, first, last, blk_dev, rows_smem, wide_ref, *refs):
    n_req = rows_smem.shape[0]
    rows = rows_smem.shape[1]
    if first:
        query_refs, refs = refs[:n_req], refs[n_req:]
    kv_refs, refs = refs[:n_buf], refs[n_buf:]
    if not first:
        refs = refs[3:]
    if last:
        out_refs, refs = refs[:n_req], refs[n_req:]
    acc_ref, top_ref, query_buf, kv_buf, score_a, score_b, best_a, best_b, item_ref, query_sem, kv_sem = refs
    tiles, half = query_buf.shape[1:3]
    query_copies = [
        pltpu.make_async_copy(ref.at[pl.ds(tile * half, half)], query_buf.at[i, tile], query_sem.at[i, tile])
        for i, ref in enumerate(query_refs)
        for tile in range(tiles)
    ] if first else []
    kv_copies = [
        pltpu.make_async_copy(ref, kv_buf.at[pl.ds(i * blk_dev, blk_dev)], kv_sem.at[i]) for i, ref in enumerate(kv_refs)
    ]
    for copy in kv_copies + query_copies:
        copy.start()
    me = lax.axis_index("shard")
    my_head, my_sub = me // n_sub, me % n_sub
    kv_local = n_req // n_sub
    mixed = my_sub * kv_local + my_head % kv_local
    block_len = kv_buf.shape[1] - TAG
    if first:
        acc_ref[...] = jnp.zeros_like(acc_ref)
        top_ref[...] = jnp.full_like(top_ref, TOP_START)
    for copy in kv_copies:
        copy.wait()
    count = jnp.int32(0)
    for i in range(n_buf * blk_dev):
        tag = kv_buf[i, block_len:, :].astype(jnp.float32)
        request = jnp.max(tag[:, :HD]).astype(jnp.int32)
        offset = jnp.max(tag[:, HD:]).astype(jnp.int32) * block_len
        for tile in reversed(range(tiles)):
            item_ref[0, count] = i
            item_ref[1, count] = request
            item_ref[2, count] = tile
            item_ref[3, count] = offset
            used = rows_smem[request, (tile + 1) * (rows // tiles) - 1] > offset
            count = count + jnp.where(used, 1, 0)
    for pad in range(2):
        item_ref[0, count + pad] = 0
        item_ref[1, count + pad] = 0
        item_ref[2, count + pad] = 0
        item_ref[3, count + pad] = NOWHERE
    for copy in query_copies:
        copy.wait()
    scale = math.log2(math.e) / math.sqrt(HD)
    token = lax.broadcasted_iota(jnp.int32, (block_len, half), 0)

    def score(item, score_ref, best_ref):
        i, request, tile = item_ref[0, item], item_ref[1, item], item_ref[2, item]
        scores = lax.dot_general(
            kv_buf[i, :block_len, :HD],
            query_buf[request ^ mixed, tile],
            (((1,), (1,)), ((), ())),
            preferred_element_type=jnp.float32,
        )
        limit = wide_ref[tile * n_req + request] - item_ref[3, item]
        scores = jnp.where(token < limit, scores * scale, MASKED)
        score_ref[...] = scores
        best_ref[...] = jnp.max(scores, axis=0, keepdims=True)

    def add(item, score_ref, best_ref):
        i = item_ref[0, item]
        place = item_ref[2, item] * n_req + item_ref[1, item]
        old_top = top_ref[place]
        new_top = jnp.maximum(old_top, best_ref[...])
        factor = jnp.exp2(old_top - new_top)
        weights = jnp.exp2(score_ref[...] - new_top).astype(jnp.bfloat16)
        values = jnp.concatenate(
            [jnp.transpose(kv_buf[i, :block_len, HD:]), jnp.ones((STATS, block_len), jnp.bfloat16)], axis=0
        )
        summed = jnp.dot(values, weights, preferred_element_type=jnp.float32)
        acc_ref[place] = acc_ref[place] * factor + summed[: HD + 8]
        top_ref[place] = new_top

    score(0, score_a, best_a)

    def two_items(j, carried):
        score(2 * j + 1, score_b, best_b)
        add(2 * j, score_a, best_a)
        score(2 * j + 2, score_a, best_a)
        add(2 * j + 1, score_b, best_b)
        return carried

    lax.fori_loop(0, (count + 1) // 2, two_items, 0)

    if last:
        for step, out_ref in enumerate(out_refs):
            request = step ^ mixed
            levels = []
            for tile in range(tiles):
                place = tile * n_req + request
                total = acc_ref[place, HD : HD + 1]
                some = total > 0.0
                safe = jnp.where(some, total, 1.0)
                result = acc_ref[place, :HD] * (1.0 / safe)
                out_ref[tile * half : (tile + 1) * half, :] = jnp.transpose(result).astype(jnp.bfloat16)
                level = jnp.where(some, top_ref[place] + jnp.log2(safe), TOP_START)
                levels += [level[:, at * HD : (at + 1) * HD] for at in range(half // HD)]
            level = jnp.concatenate(levels, axis=0)
            high = level.astype(jnp.bfloat16)
            rest = level - high.astype(jnp.float32)
            middle = rest.astype(jnp.bfloat16)
            low = (rest - middle.astype(jnp.float32)).astype(jnp.bfloat16)
            pieces = [high, middle, low, jnp.zeros((STATS - 3 * len(levels), HD), jnp.bfloat16)]
            out_ref[tiles * half :, :] = jnp.concatenate(pieces, axis=0)


def own_scores(n_sub, group_size, rows_ref, fresh_ref, *refs):
    query_refs, own_ref, wide_ref = refs[:-2], refs[-2], refs[-1]
    request = lax.axis_index("shard") // n_sub
    n_req, rows = rows_ref.shape
    kv_local = fresh_ref.shape[1] // (2 * HD)
    sub_heads = group_size // n_sub
    lines = sub_heads * rows // HD
    scale = math.log2(math.e) / math.sqrt(HD)
    own_ref[...] = jnp.zeros_like(own_ref)
    cosine, sine = row_turns(rows_ref[pl.ds(request, 1), :])
    for step, query_ref in enumerate(query_refs):
        kv_id = (step % kv_local) ^ (request % kv_local)
        column = pl.multiple_of(2 * kv_id * HD, HD)
        own_key = turn(fresh_ref[:, pl.ds(column, HD)], cosine, sine).astype(jnp.float32)
        for head, row_part, flat in chunks_of(sub_heads, rows):
            query = query_ref[flat, :].astype(jnp.float32)
            line, at = step * lines + flat.start // HD, flat.start % HD
            own = jnp.sum(query * own_key[row_part, :], axis=1, keepdims=True) * scale
            own_ref[at : at + own.shape[0], line : line + 1] = own
    tiles = tiles_of(sub_heads * rows)
    size = rows // tiles
    for tile in range(tiles):
        wide = jnp.concatenate([rows_ref[:, tile * size : (tile + 1) * size]] * sub_heads, axis=1)
        for r in range(n_req):
            wide_ref[tile * n_req + r] = wide[r : r + 1]


def merge_own(n_sub, group_size, own_ref, fresh_ref, *refs):
    part_refs, out_ref, level_ref = refs[:-2], refs[-2], refs[-1]
    request = lax.axis_index("shard") // n_sub
    rows = out_ref.shape[0]
    kv_local = fresh_ref.shape[1] // (2 * HD)
    sub_heads = group_size // n_sub
    width = sub_heads * rows
    lines = width // HD
    level_ref[...] = jnp.zeros_like(level_ref)
    for step, part_ref in enumerate(part_refs):
        stats = part_ref[width:, :].astype(jnp.float32)
        level_ref[step * lines : (step + 1) * lines] = stats[:lines] + stats[lines : 2 * lines] + stats[2 * lines : 3 * lines]
    level = jnp.transpose(level_ref[...])
    own = own_ref[...]
    top = jnp.maximum(own, level)
    own_share = jnp.exp2(own - top)
    share = jnp.exp2(level - top)
    norm = 1.0 / (own_share + share)
    own_share, share = own_share * norm, share * norm
    for step, part_ref in enumerate(part_refs):
        kv_id = (step % kv_local) ^ (request % kv_local)
        sub = (step // kv_local) ^ (request // kv_local)
        value_column = pl.multiple_of((2 * kv_id + 1) * HD, HD)
        own_value = fresh_ref[:, pl.ds(value_column, HD)].astype(jnp.float32)
        for head, row_part, flat in chunks_of(sub_heads, rows):
            line, at = step * lines + flat.start // HD, flat.start % HD
            size = flat.stop - flat.start
            part = part_ref[flat, :].astype(jnp.float32)
            column = pl.multiple_of((kv_id * group_size + sub * sub_heads + head) * HD, HD)
            out_ref[row_part, pl.ds(column, HD)] = (
                part * share[at : at + size, line : line + 1]
                + own_value[row_part, :] * own_share[at : at + size, line : line + 1]
            ).astype(jnp.bfloat16)


def moved(x, pairs):
    return lax.ppermute(x, "shard", pairs)


def shards(kv_store, block_order, lengths, row_positions, queries, fresh_rows):
    n_shard = lax.axis_size("shard")
    n_req, rows = row_positions.shape
    n_sub = n_shard // n_req
    blk_dev, block_len, full_width = kv_store.shape
    kv_heads = full_width // (2 * HD)
    kv_local = kv_heads // n_sub
    group_size = queries.shape[1] // (kv_local * HD)
    sub_heads = group_size // n_sub
    width = sub_heads * rows
    tiles = tiles_of(width)
    half_width = width // tiles
    bf16 = jnp.bfloat16
    spec = functools.partial(pl.BlockSpec, memory_space=VMEM)
    smem = pl.BlockSpec(memory_space=SMEM)
    anywhere = pl.BlockSpec(memory_space=pl.ANY)

    grant = pltpu.CompilerParams(vmem_limit_bytes=GRANT)
    sent_queries = pl.pallas_call(
        functools.partial(pack_queries, n_sub, group_size),
        out_shape=[jax.ShapeDtypeStruct((width, HD), bf16)] * n_req,
        in_specs=[anywhere] * 2,
        out_specs=[spec()] * n_req,
        scratch_shapes=[
            pltpu.VMEM((rows, HD), jnp.float32),
            pltpu.VMEM((rows, HD), jnp.float32),
            pltpu.VMEM((n_req, rows), jnp.int32),
            pltpu.VMEM((kv_local, rows, group_size * HD), bf16),
            pltpu.SemaphoreType.DMA((kv_local + 1,)),
        ],
        compiler_params=grant,
        name="pack_queries",
    )(row_positions, queries)
    level_rows = max(HD, n_req * width // HD)
    own, wide_rows = pl.pallas_call(
        functools.partial(own_scores, n_sub, group_size),
        out_shape=[
            jax.ShapeDtypeStruct((rows, level_rows), jnp.float32),
            jax.ShapeDtypeStruct((n_req * tiles, 1, width // tiles), jnp.int32),
        ],
        in_specs=[spec()] * (2 + n_req),
        out_specs=[spec()] * 2,
        compiler_params=grant,
        name="own_scores",
    )(row_positions, fresh_rows, *sent_queries)
    lengths_after = lax.optimization_barrier((lengths, sent_queries[0]))[0]

    packed_kv = pl.pallas_call(
        functools.partial(pack_kv, n_sub),
        out_shape=[jax.ShapeDtypeStruct((blk_dev, block_len + TAG, 2 * HD), bf16)] * kv_heads,
        in_specs=[smem, smem, anywhere],
        out_specs=[spec()] * kv_heads,
        scratch_shapes=[pltpu.VMEM((blk_dev, block_len, full_width), bf16), pltpu.SemaphoreType.DMA((blk_dev,))],
        compiler_params=grant,
        name="pack_kv",
    )(block_order, lengths_after, kv_store)

    to_compute = []
    for step in range(n_req):
        pairs = []
        for request in range(n_req):
            for h in range(n_sub):
                head = kv_local * h + ((step % kv_local) ^ (request % kv_local))
                sub = (step // kv_local) ^ (request // kv_local)
                pairs.append((request * n_sub + h, head * n_sub + sub))
        to_compute.append(pairs)
    held_queries = [moved(x, pairs) for x, pairs in zip(sent_queries, to_compute)]


    def after(x, *others):
        return lax.optimization_barrier((x, *others))[0] if others else x

    def at_head(mask, *others):
        pairs = [(d, ((d // n_sub) ^ mask) * n_sub + d % n_sub) for d in range(n_shard)]
        return packed_kv[0] if mask == 0 else moved(after(packed_kv[mask], *others), pairs)

    def from_sub(mask, back, *others):
        x = landed[mask]
        pairs = [(d, (d // n_sub) * n_sub + (d % n_sub + back) % n_sub) for d in range(n_shard)]
        return x if back == 0 else moved(after(x, *others), pairs)

    half = kv_heads // 2
    groups = [[0], list(range(1, half)), [half, half + 1]] + [[mask] for mask in range(half + 2, kv_heads)]
    landed = {mask: at_head(mask) for mask in range(half + 2)}
    landed[half + 2] = at_head(half + 2, *held_queries)
    state_shapes = [
        pltpu.VMEM((n_req * tiles, HD + 8, half_width), jnp.float32),
        pltpu.VMEM((n_req * tiles, 1, half_width), jnp.float32),
        pltpu.VMEM((n_req, tiles, half_width, HD), bf16),
    ]
    part_shapes = [jax.ShapeDtypeStruct((width + STATS, HD), bf16)] * n_req
    state = []
    for index, masks in enumerate(groups):
        if index == 1:
            for mask in range(half + 3, kv_heads):
                if mask not in landed:
                    landed[mask] = at_head(mask, landed[half])
        arrived = [from_sub(mask, back, *state[-1:]) for mask in masks for back in range(n_sub)]
        buffers = [(mask, back) for mask in masks for back in range(n_sub)]
        first, last = index == 0, index == len(groups) - 1
        blocks = len(buffers) * blk_dev
        inputs = [*(held_queries if first else []), *arrived]
        results = pl.pallas_call(
            functools.partial(attend, n_sub, len(buffers), first, last, blk_dev),
            out_shape=(part_shapes if last else []) + state_shapes,
            in_specs=[smem, spec()] + [anywhere] * len(inputs) + [spec()] * len(state),
            out_specs=[spec()] * ((n_req if last else 0) + 3),
            input_output_aliases={2 + len(inputs) + k: (n_req if last else 0) + k for k in range(len(state))},
            scratch_shapes=[
                pltpu.VMEM((blocks, block_len + TAG, 2 * HD), bf16),
                pltpu.VMEM((block_len, half_width), jnp.float32),
                pltpu.VMEM((block_len, half_width), jnp.float32),
                pltpu.VMEM((1, half_width), jnp.float32),
                pltpu.VMEM((1, half_width), jnp.float32),
                pltpu.SMEM((4, blocks * tiles + 2), jnp.int32),
                pltpu.SemaphoreType.DMA((n_req, tiles)),
                pltpu.SemaphoreType.DMA((len(buffers),)),
            ],
            compiler_params=grant,
        )(row_positions, wide_rows, *inputs, *state)
        state = list(results)
    returned = [moved(part, [(b, a) for a, b in pairs]) for part, pairs in zip(state, to_compute)]

    return pl.pallas_call(
        functools.partial(merge_own, n_sub, group_size),
        out_shape=jax.ShapeDtypeStruct((rows, kv_local * group_size * HD), bf16),
        in_specs=[spec()] * (2 + n_req),
        out_specs=spec(),
        scratch_shapes=[pltpu.VMEM((level_rows, rows), jnp.float32)],
        compiler_params=grant,
        name="merge_own",
    )(own, fresh_rows, *returned)


def solution(mesh):
    in_specs = (
        P(("groups", "shard"), None, None),
        P(("groups", "shard")),
        P("groups"),
        P("groups", None),
        P("groups", "shard"),
        P("groups", "shard"),
    )
    return jax.shard_map(shards, mesh=mesh, in_specs=in_specs, out_specs=P("groups", "shard"), check_vma=False)
```

```python
import functools
import math

import jax
import jax.numpy as jnp
from jax import lax
from jax.experimental import pallas as pl
from jax.experimental.pallas import tpu as pltpu
from jax.sharding import PartitionSpec as P


HD = 128
ROPE_BASE = 500000.0
TOP_START = -1e30
MASKED = -3e30
STATS = 16
TAG = 8
NOWHERE = 1 << 28
GRANT = 24 << 20


def tiles_of(width):
    return 2 if width % (4 * HD) == 0 else 1


def chunks_of(sub_heads, rows):
    tiles = tiles_of(sub_heads * rows)
    size = rows // tiles
    for tile in range(tiles):
        for head in range(sub_heads):
            start = (tile * sub_heads + head) * size
            yield head, slice(tile * size, (tile + 1) * size), slice(start, start + size)


VMEM = pltpu.MemorySpace.VMEM
SMEM = pltpu.MemorySpace.SMEM


def frequencies():
    half = HD // 2
    steps = lax.broadcasted_iota(jnp.int32, (1, HD), 1) % half
    return jnp.exp(-math.log(ROPE_BASE) * steps.astype(jnp.float32) / half)


def signed(sine):
    lane = lax.broadcasted_iota(jnp.int32, sine.shape, len(sine.shape) - 1)
    return jnp.where(lane < HD // 2, -sine, sine)


def turn(vectors, cosine, sine):
    wide = vectors.astype(jnp.float32)
    return (wide * cosine + pltpu.roll(wide, HD // 2, 1) * sine).astype(jnp.bfloat16)


def find_block(block_id, lengths_ref):
    start = jnp.int32(0)
    request = jnp.int32(0)
    position = jnp.int32(0)
    for q in range(lengths_ref.shape[0]):
        end = start + lengths_ref[q]
        inside = (block_id >= start) & (block_id < end)
        request = jnp.where(inside, q, request)
        position = jnp.where(inside, block_id - start, position)
        start = end
    return request, position


def pack_kv(n_sub, order_ref, lengths_ref, kv_ref, *refs):
    out_refs, buf, sem = refs[:-2], refs[-2], refs[-1]
    heads = len(out_refs)
    slots = buf.shape[0]
    copies = [pltpu.make_async_copy(kv_ref.at[slot], buf.at[slot], sem.at[slot]) for slot in range(slots)]
    for copy in copies:
        copy.start()
    my_head = lax.axis_index("shard") // n_sub
    block_len = buf.shape[1]
    tags = TAG // slots
    left = lax.broadcasted_iota(jnp.int32, (tags, 2 * HD), 1) < HD
    for slot in range(slots):
        request, position = find_block(order_ref[slot], lengths_ref)
        tag = jnp.where(left, request, position).astype(jnp.float32).astype(jnp.bfloat16)
        tokens = slice(slot * block_len, (slot + 1) * block_len)
        angle = (position * block_len).astype(jnp.float32) * frequencies()
        cosine, sine = jnp.cos(angle), signed(jnp.sin(angle))
        copies[slot].wait()
        for mask in range(heads):
            column = pl.multiple_of((my_head ^ mask) * (2 * HD), 2 * HD)
            out_refs[mask][tokens, :HD] = turn(buf[slot, :, pl.ds(column, HD)], cosine, sine)
            out_refs[mask][tokens, HD:] = buf[slot, :, pl.ds(column + HD, HD)]
            first_tag = slots * block_len + slot * tags
            out_refs[mask][first_tag : first_tag + tags, :] = tag


def row_turns(row):
    angle = jnp.transpose(jnp.broadcast_to(row.astype(jnp.float32), (HD, row.shape[1]))) * frequencies()
    return jnp.cos(angle), signed(jnp.sin(angle))


def pack_queries(n_sub, group_size, rows_ref, queries_ref, *refs):
    out_refs, (cos_ref, sin_ref, rows_buf, buf, sem) = refs[:-5], refs[-5:]
    request = lax.axis_index("shard") // n_sub
    kv_local = buf.shape[0]
    rows = buf.shape[1]
    span = group_size * HD
    rows_copy = pltpu.make_async_copy(rows_ref, rows_buf, sem.at[kv_local])
    rows_copy.start()
    copies = [
        pltpu.make_async_copy(queries_ref.at[:, pl.ds(kv_id * span, span)], buf.at[kv_id], sem.at[kv_id])
        for kv_id in range(kv_local)
    ]
    for copy in copies:
        copy.start()
    sub_heads = group_size // n_sub
    rows_copy.wait()
    cos_ref[...], sin_ref[...] = row_turns(rows_buf[pl.ds(request, 1), :])
    for copy in copies:
        copy.wait()
    for step, out_ref in enumerate(out_refs):
        kv_id = (step % kv_local) ^ (request % kv_local)
        sub = (step // kv_local) ^ (request // kv_local)
        for head, row_part, flat in chunks_of(sub_heads, rows):
            column = pl.multiple_of((sub * sub_heads + head) * HD, HD)
            out_ref[flat, :] = turn(buf[kv_id, row_part, pl.ds(column, HD)], cos_ref[row_part, :], sin_ref[row_part, :])


def attend(n_sub, n_buf, first, last, blk_dev, rows_smem, wide_ref, *refs):
    n_req = rows_smem.shape[0]
    rows = rows_smem.shape[1]
    if first:
        query_refs, refs = refs[:n_req], refs[n_req:]
    kv_refs, refs = refs[:n_buf], refs[n_buf:]
    if not first:
        refs = refs[3:]
    if last:
        out_refs, refs = refs[:n_req], refs[n_req:]
    acc_ref, top_ref, query_buf, kv_buf, score_a, score_b, best_a, best_b, item_ref, query_sem, kv_sem = refs
    tiles, half = query_buf.shape[1:3]
    query_copies = [
        pltpu.make_async_copy(ref.at[pl.ds(tile * half, half)], query_buf.at[i, tile], query_sem.at[i, tile])
        for i, ref in enumerate(query_refs)
        for tile in range(tiles)
    ] if first else []
    kv_copies = [
        pltpu.make_async_copy(ref, kv_buf.at[i], kv_sem.at[i]) for i, ref in enumerate(kv_refs)
    ]
    for copy in kv_copies + query_copies:
        copy.start()
    me = lax.axis_index("shard")
    my_head, my_sub = me // n_sub, me % n_sub
    kv_local = n_req // n_sub
    mixed = my_sub * kv_local + my_head % kv_local
    block_len = (kv_buf.shape[1] - TAG) // blk_dev
    tags = TAG // blk_dev
    if first:
        acc_ref[...] = jnp.zeros_like(acc_ref)
        top_ref[...] = jnp.full_like(top_ref, TOP_START)
    for copy in kv_copies:
        copy.wait()
    count = jnp.int32(0)
    for i in range(n_buf * blk_dev):
        first_tag = blk_dev * block_len + (i % blk_dev) * tags
        tag = kv_buf[i // blk_dev, first_tag : first_tag + tags, :].astype(jnp.float32)
        request = jnp.max(tag[:, :HD]).astype(jnp.int32)
        offset = jnp.max(tag[:, HD:]).astype(jnp.int32) * block_len
        for tile in reversed(range(tiles)):
            item_ref[0, count] = i // blk_dev
            item_ref[4, count] = (i % blk_dev) * block_len
            item_ref[1, count] = request
            item_ref[2, count] = tile
            item_ref[3, count] = offset
            used = rows_smem[request, (tile + 1) * (rows // tiles) - 1] > offset
            count = count + jnp.where(used, 1, 0)
    for pad in range(2):
        item_ref[0, count + pad] = 0
        item_ref[4, count + pad] = 0
        item_ref[1, count + pad] = 0
        item_ref[2, count + pad] = 0
        item_ref[3, count + pad] = NOWHERE
    for copy in query_copies:
        copy.wait()
    scale = math.log2(math.e) / math.sqrt(HD)
    token = lax.broadcasted_iota(jnp.int32, (block_len, half), 0)

    def tokens_of(item):
        return pl.ds(pl.multiple_of(item_ref[4, item], 8), block_len)

    def score(item, score_ref, best_ref):
        i, request, tile = item_ref[0, item], item_ref[1, item], item_ref[2, item]
        scores = lax.dot_general(
            kv_buf[i, tokens_of(item), :HD],
            query_buf[request ^ mixed, tile],
            (((1,), (1,)), ((), ())),
            preferred_element_type=jnp.float32,
        )
        limit = wide_ref[tile * n_req + request] - item_ref[3, item]
        scores = jnp.where(token < limit, scores * scale, MASKED)
        score_ref[...] = scores
        best_ref[...] = jnp.max(scores, axis=0, keepdims=True)

    def add(item, score_ref, best_ref):
        i = item_ref[0, item]
        place = item_ref[2, item] * n_req + item_ref[1, item]
        old_top = top_ref[place]
        new_top = jnp.maximum(old_top, best_ref[...])
        factor = jnp.exp2(old_top - new_top)
        weights = jnp.exp2(score_ref[...] - new_top).astype(jnp.bfloat16)
        values = jnp.concatenate(
            [jnp.transpose(kv_buf[i, tokens_of(item), HD:]), jnp.ones((STATS, block_len), jnp.bfloat16)], axis=0
        )
        summed = jnp.dot(values, weights, preferred_element_type=jnp.float32)
        acc_ref[place] = acc_ref[place] * factor + summed[: HD + 8]
        top_ref[place] = new_top

    score(0, score_a, best_a)

    def two_items(j, carried):
        score(2 * j + 1, score_b, best_b)
        add(2 * j, score_a, best_a)
        score(2 * j + 2, score_a, best_a)
        add(2 * j + 1, score_b, best_b)
        return carried

    lax.fori_loop(0, (count + 1) // 2, two_items, 0)

    if last:
        for step, out_ref in enumerate(out_refs):
            request = step ^ mixed
            levels = []
            for tile in range(tiles):
                place = tile * n_req + request
                total = acc_ref[place, HD : HD + 1]
                some = total > 0.0
                safe = jnp.where(some, total, 1.0)
                result = acc_ref[place, :HD] * (1.0 / safe)
                out_ref[tile * half : (tile + 1) * half, :] = jnp.transpose(result).astype(jnp.bfloat16)
                level = jnp.where(some, top_ref[place] + jnp.log2(safe), TOP_START)
                levels += [level[:, at * HD : (at + 1) * HD] for at in range(half // HD)]
            level = jnp.concatenate(levels, axis=0)
            high = level.astype(jnp.bfloat16)
            rest = level - high.astype(jnp.float32)
            middle = rest.astype(jnp.bfloat16)
            low = (rest - middle.astype(jnp.float32)).astype(jnp.bfloat16)
            pieces = [high, middle, low, jnp.zeros((STATS - 3 * len(levels), HD), jnp.bfloat16)]
            out_ref[tiles * half :, :] = jnp.concatenate(pieces, axis=0)


def own_scores(n_sub, group_size, rows_ref, fresh_ref, *refs):
    query_refs, own_ref, wide_ref = refs[:-2], refs[-2], refs[-1]
    request = lax.axis_index("shard") // n_sub
    n_req, rows = rows_ref.shape
    kv_local = fresh_ref.shape[1] // (2 * HD)
    sub_heads = group_size // n_sub
    lines = sub_heads * rows // HD
    scale = math.log2(math.e) / math.sqrt(HD)
    own_ref[...] = jnp.zeros_like(own_ref)
    cosine, sine = row_turns(rows_ref[pl.ds(request, 1), :])
    for step, query_ref in enumerate(query_refs):
        kv_id = (step % kv_local) ^ (request % kv_local)
        column = pl.multiple_of(2 * kv_id * HD, HD)
        own_key = turn(fresh_ref[:, pl.ds(column, HD)], cosine, sine).astype(jnp.float32)
        for head, row_part, flat in chunks_of(sub_heads, rows):
            query = query_ref[flat, :].astype(jnp.float32)
            line, at = step * lines + flat.start // HD, flat.start % HD
            own = jnp.sum(query * own_key[row_part, :], axis=1, keepdims=True) * scale
            own_ref[at : at + own.shape[0], line : line + 1] = own
    tiles = tiles_of(sub_heads * rows)
    size = rows // tiles
    for tile in range(tiles):
        wide = jnp.concatenate([rows_ref[:, tile * size : (tile + 1) * size]] * sub_heads, axis=1)
        for r in range(n_req):
            wide_ref[tile * n_req + r] = wide[r : r + 1]


def merge_own(n_sub, group_size, own_ref, fresh_ref, *refs):
    part_refs, (out_ref, level_ref, out_buf, out_sem) = refs[:-4], refs[-4:]
    request = lax.axis_index("shard") // n_sub
    rows = out_ref.shape[0]
    copies = []
    kv_local = fresh_ref.shape[1] // (2 * HD)
    sub_heads = group_size // n_sub
    width = sub_heads * rows
    lines = width // HD
    level_ref[...] = jnp.zeros_like(level_ref)
    for step, part_ref in enumerate(part_refs):
        stats = part_ref[width:, :].astype(jnp.float32)
        level_ref[step * lines : (step + 1) * lines] = stats[:lines] + stats[lines : 2 * lines] + stats[2 * lines : 3 * lines]
    level = jnp.transpose(level_ref[...])
    own = own_ref[...]
    top = jnp.maximum(own, level)
    own_share = jnp.exp2(own - top)
    share = jnp.exp2(level - top)
    norm = 1.0 / (own_share + share)
    own_share, share = own_share * norm, share * norm
    for step, part_ref in enumerate(part_refs):
        kv_id = (step % kv_local) ^ (request % kv_local)
        sub = (step // kv_local) ^ (request // kv_local)
        value_column = pl.multiple_of((2 * kv_id + 1) * HD, HD)
        own_value = fresh_ref[:, pl.ds(value_column, HD)].astype(jnp.float32)
        for head, row_part, flat in chunks_of(sub_heads, rows):
            line, at = step * lines + flat.start // HD, flat.start % HD
            size = flat.stop - flat.start
            part = part_ref[flat, :].astype(jnp.float32)
            out_buf[step, row_part, head * HD : (head + 1) * HD] = (
                part * share[at : at + size, line : line + 1]
                + own_value[row_part, :] * own_share[at : at + size, line : line + 1]
            ).astype(jnp.bfloat16)
        span = sub_heads * HD
        column = pl.multiple_of((kv_id * group_size + sub * sub_heads) * HD, HD)
        copies.append(pltpu.make_async_copy(out_buf.at[step], out_ref.at[:, pl.ds(column, span)], out_sem.at[step]))
        copies[-1].start()
    for copy in copies:
        copy.wait()


def moved(x, pairs):
    return lax.ppermute(x, "shard", pairs)


def shards(kv_store, block_order, lengths, row_positions, queries, fresh_rows):
    n_shard = lax.axis_size("shard")
    n_req, rows = row_positions.shape
    n_sub = n_shard // n_req
    blk_dev, block_len, full_width = kv_store.shape
    kv_heads = full_width // (2 * HD)
    kv_local = kv_heads // n_sub
    group_size = queries.shape[1] // (kv_local * HD)
    sub_heads = group_size // n_sub
    width = sub_heads * rows
    tiles = tiles_of(width)
    half_width = width // tiles
    bf16 = jnp.bfloat16
    spec = functools.partial(pl.BlockSpec, memory_space=VMEM)
    smem = pl.BlockSpec(memory_space=SMEM)
    anywhere = pl.BlockSpec(memory_space=pl.ANY)

    grant = pltpu.CompilerParams(vmem_limit_bytes=GRANT)
    sent_queries = pl.pallas_call(
        functools.partial(pack_queries, n_sub, group_size),
        out_shape=[jax.ShapeDtypeStruct((width, HD), bf16)] * n_req,
        in_specs=[anywhere] * 2,
        out_specs=[spec()] * n_req,
        scratch_shapes=[
            pltpu.VMEM((rows, HD), jnp.float32),
            pltpu.VMEM((rows, HD), jnp.float32),
            pltpu.VMEM((n_req, rows), jnp.int32),
            pltpu.VMEM((kv_local, rows, group_size * HD), bf16),
            pltpu.SemaphoreType.DMA((kv_local + 1,)),
        ],
        compiler_params=grant,
        name="pack_queries",
    )(row_positions, queries)
    level_rows = max(HD, n_req * width // HD)
    own, wide_rows = pl.pallas_call(
        functools.partial(own_scores, n_sub, group_size),
        out_shape=[
            jax.ShapeDtypeStruct((rows, level_rows), jnp.float32),
            jax.ShapeDtypeStruct((n_req * tiles, 1, width // tiles), jnp.int32),
        ],
        in_specs=[spec()] * (2 + n_req),
        out_specs=[spec()] * 2,
        compiler_params=grant,
        name="own_scores",
    )(row_positions, fresh_rows, *sent_queries)
    lengths_after = lax.optimization_barrier((lengths, sent_queries[0]))[0]

    packed_kv = pl.pallas_call(
        functools.partial(pack_kv, n_sub),
        out_shape=[jax.ShapeDtypeStruct((blk_dev * block_len + TAG, 2 * HD), bf16)] * kv_heads,
        in_specs=[smem, smem, anywhere],
        out_specs=[spec()] * kv_heads,
        scratch_shapes=[pltpu.VMEM((blk_dev, block_len, full_width), bf16), pltpu.SemaphoreType.DMA((blk_dev,))],
        compiler_params=grant,
        name="pack_kv",
    )(block_order, lengths_after, kv_store)

    to_compute = []
    for step in range(n_req):
        pairs = []
        for request in range(n_req):
            for h in range(n_sub):
                head = kv_local * h + ((step % kv_local) ^ (request % kv_local))
                sub = (step // kv_local) ^ (request // kv_local)
                pairs.append((request * n_sub + h, head * n_sub + sub))
        to_compute.append(pairs)
    held_queries = [moved(x, pairs) for x, pairs in zip(sent_queries, to_compute)]


    def after(x, *others):
        return lax.optimization_barrier((x, *others))[0] if others else x

    def at_head(mask, *others):
        pairs = [(d, ((d // n_sub) ^ mask) * n_sub + d % n_sub) for d in range(n_shard)]
        return packed_kv[0] if mask == 0 else moved(after(packed_kv[mask], *others), pairs)

    def from_sub(mask, back, *others):
        x = landed[mask]
        pairs = [(d, (d // n_sub) * n_sub + (d % n_sub + back) % n_sub) for d in range(n_shard)]
        return x if back == 0 else moved(after(x, *others), pairs)

    half = kv_heads // 2
    groups = [[0], list(range(1, half)), [half, half + 1]] + [[mask] for mask in range(half + 2, kv_heads)]
    landed = {mask: at_head(mask) for mask in range(half + 2)}
    landed[half + 2] = at_head(half + 2, *held_queries)
    state_shapes = [
        pltpu.VMEM((n_req * tiles, HD + 8, half_width), jnp.float32),
        pltpu.VMEM((n_req * tiles, 1, half_width), jnp.float32),
        pltpu.VMEM((n_req, tiles, half_width, HD), bf16),
    ]
    part_shapes = [jax.ShapeDtypeStruct((width + STATS, HD), bf16)] * n_req
    state = []
    for index, masks in enumerate(groups):
        if index == 1:
            for mask in range(half + 3, kv_heads):
                if mask not in landed:
                    landed[mask] = at_head(mask, landed[half])
        arrived = [from_sub(mask, back, *state[-1:]) for mask in masks for back in range(n_sub)]
        buffers = [(mask, back) for mask in masks for back in range(n_sub)]
        first, last = index == 0, index == len(groups) - 1
        blocks = len(buffers) * blk_dev
        inputs = [*(held_queries if first else []), *arrived]
        results = pl.pallas_call(
            functools.partial(attend, n_sub, len(buffers), first, last, blk_dev),
            out_shape=(part_shapes if last else []) + state_shapes,
            in_specs=[smem, spec()] + [anywhere] * len(inputs) + [spec()] * len(state),
            out_specs=[spec()] * ((n_req if last else 0) + 3),
            input_output_aliases={2 + len(inputs) + k: (n_req if last else 0) + k for k in range(len(state))},
            scratch_shapes=[
                pltpu.VMEM((len(buffers), blk_dev * block_len + TAG, 2 * HD), bf16),
                pltpu.VMEM((block_len, half_width), jnp.float32),
                pltpu.VMEM((block_len, half_width), jnp.float32),
                pltpu.VMEM((1, half_width), jnp.float32),
                pltpu.VMEM((1, half_width), jnp.float32),
                pltpu.SMEM((5, blocks * tiles + 2), jnp.int32),
                pltpu.SemaphoreType.DMA((n_req, tiles)),
                pltpu.SemaphoreType.DMA((len(buffers),)),
            ],
            compiler_params=grant,
        )(row_positions, wide_rows, *inputs, *state)
        state = list(results)
    returned = [moved(part, [(b, a) for a, b in pairs]) for part, pairs in zip(state, to_compute)]

    return pl.pallas_call(
        functools.partial(merge_own, n_sub, group_size),
        out_shape=jax.ShapeDtypeStruct((rows, kv_local * group_size * HD), bf16),
        in_specs=[spec()] * (2 + n_req),
        out_specs=anywhere,
        scratch_shapes=[
            pltpu.VMEM((level_rows, rows), jnp.float32),
            pltpu.VMEM((n_req, rows, sub_heads * HD), bf16),
            pltpu.SemaphoreType.DMA((n_req,)),
        ],
        compiler_params=grant,
        name="merge_own",
    )(own, fresh_rows, *returned)


def solution(mesh):
    in_specs = (
        P(("groups", "shard"), None, None),
        P(("groups", "shard")),
        P("groups"),
        P("groups", None),
        P("groups", "shard"),
        P("groups", "shard"),
    )
    return jax.shard_map(shards, mesh=mesh, in_specs=in_specs, out_specs=P("groups", "shard"), check_vma=False)
```

```python
import functools
import math

import jax
import jax.numpy as jnp
from jax import lax
from jax.experimental import pallas as pl
from jax.experimental.pallas import tpu as pltpu
from jax.sharding import PartitionSpec as P


HD = 128
ROPE_BASE = 500000.0
TOP_START = -1e30
MASKED = -3e30
STATS = 16
TAG = 8
NOWHERE = 1 << 28
GRANT = 24 << 20


def tiles_of(width):
    return 2 if width % (4 * HD) == 0 else 1


def chunks_of(sub_heads, rows):
    tiles = tiles_of(sub_heads * rows)
    size = rows // tiles
    for tile in range(tiles):
        for head in range(sub_heads):
            start = (tile * sub_heads + head) * size
            yield head, slice(tile * size, (tile + 1) * size), slice(start, start + size)


VMEM = pltpu.MemorySpace.VMEM
SMEM = pltpu.MemorySpace.SMEM


def frequencies():
    half = HD // 2
    steps = lax.broadcasted_iota(jnp.int32, (1, HD), 1) % half
    return jnp.exp(-math.log(ROPE_BASE) * steps.astype(jnp.float32) / half)


def signed(sine):
    lane = lax.broadcasted_iota(jnp.int32, sine.shape, len(sine.shape) - 1)
    return jnp.where(lane < HD // 2, -sine, sine)


def turn(vectors, cosine, sine):
    wide = vectors.astype(jnp.float32)
    return (wide * cosine + pltpu.roll(wide, HD // 2, 1) * sine).astype(jnp.bfloat16)


def find_block(block_id, lengths_ref):
    start = jnp.int32(0)
    request = jnp.int32(0)
    position = jnp.int32(0)
    for q in range(lengths_ref.shape[0]):
        end = start + lengths_ref[q]
        inside = (block_id >= start) & (block_id < end)
        request = jnp.where(inside, q, request)
        position = jnp.where(inside, block_id - start, position)
        start = end
    return request, position


def pack_kv(n_sub, order_ref, lengths_ref, kv_ref, *refs):
    out_refs, buf, sem = refs[:-2], refs[-2], refs[-1]
    heads = len(out_refs)
    slots = buf.shape[0]
    copies = [pltpu.make_async_copy(kv_ref.at[slot], buf.at[slot], sem.at[slot]) for slot in range(slots)]
    for copy in copies:
        copy.start()
    my_head = lax.axis_index("shard") // n_sub
    block_len = buf.shape[1]
    tags = TAG // slots
    left = lax.broadcasted_iota(jnp.int32, (tags, 2 * HD), 1) < HD
    for slot in range(slots):
        request, position = find_block(order_ref[slot], lengths_ref)
        tag = jnp.where(left, request, position).astype(jnp.float32).astype(jnp.bfloat16)
        tokens = slice(slot * block_len, (slot + 1) * block_len)
        angle = (position * block_len).astype(jnp.float32) * frequencies()
        cosine, sine = jnp.cos(angle), signed(jnp.sin(angle))
        copies[slot].wait()
        for mask in range(heads):
            column = pl.multiple_of((my_head ^ mask) * (2 * HD), 2 * HD)
            out_refs[mask][tokens, :HD] = turn(buf[slot, :, pl.ds(column, HD)], cosine, sine)
            out_refs[mask][tokens, HD:] = buf[slot, :, pl.ds(column + HD, HD)]
            first_tag = slots * block_len + slot * tags
            out_refs[mask][first_tag : first_tag + tags, :] = tag


def row_turns(row):
    angle = jnp.transpose(jnp.broadcast_to(row.astype(jnp.float32), (HD, row.shape[1]))) * frequencies()
    return jnp.cos(angle), signed(jnp.sin(angle))


def pack_queries(n_sub, group_size, rows_ref, queries_ref, *refs):
    out_refs, (cos_ref, sin_ref, rows_buf, buf, sem) = refs[:-5], refs[-5:]
    request = lax.axis_index("shard") // n_sub
    kv_local = buf.shape[0]
    rows = buf.shape[1]
    span = group_size * HD
    rows_copy = pltpu.make_async_copy(rows_ref, rows_buf, sem.at[kv_local])
    rows_copy.start()
    copies = [
        pltpu.make_async_copy(queries_ref.at[:, pl.ds(kv_id * span, span)], buf.at[kv_id], sem.at[kv_id])
        for kv_id in range(kv_local)
    ]
    for copy in copies:
        copy.start()
    sub_heads = group_size // n_sub
    rows_copy.wait()
    cos_ref[...], sin_ref[...] = row_turns(rows_buf[pl.ds(request, 1), :])
    for copy in copies:
        copy.wait()
    for step, out_ref in enumerate(out_refs):
        kv_id = (step % kv_local) ^ (request % kv_local)
        sub = (step // kv_local) ^ (request // kv_local)
        for head, row_part, flat in chunks_of(sub_heads, rows):
            column = pl.multiple_of((sub * sub_heads + head) * HD, HD)
            out_ref[flat, :] = turn(buf[kv_id, row_part, pl.ds(column, HD)], cos_ref[row_part, :], sin_ref[row_part, :])


def attend(n_sub, n_buf, first, last, blk_dev, rows_smem, wide_ref, *refs):
    n_req = rows_smem.shape[0]
    rows = rows_smem.shape[1]
    if first:
        query_refs, refs = refs[:n_req], refs[n_req:]
    kv_refs, refs = refs[:n_buf], refs[n_buf:]
    if not first:
        refs = refs[3:]
    if last:
        out_refs, refs = refs[:n_req], refs[n_req:]
    acc_ref, top_ref, query_buf, kv_buf, score_a, score_b, best_a, best_b, item_ref, query_sem, kv_sem = refs
    tiles, half = query_buf.shape[1:3]
    query_copies = [
        pltpu.make_async_copy(ref.at[pl.ds(tile * half, half)], query_buf.at[i, tile], query_sem.at[i, tile])
        for i, ref in enumerate(query_refs)
        for tile in range(tiles)
    ] if first else []
    kv_copies = [
        pltpu.make_async_copy(ref, kv_buf.at[i], kv_sem.at[i]) for i, ref in enumerate(kv_refs)
    ]
    for copy in kv_copies + query_copies:
        copy.start()
    me = lax.axis_index("shard")
    my_head, my_sub = me // n_sub, me % n_sub
    kv_local = n_req // n_sub
    mixed = my_sub * kv_local + my_head % kv_local
    block_len = (kv_buf.shape[1] - TAG) // blk_dev
    tags = TAG // blk_dev
    if first:
        acc_ref[...] = jnp.zeros_like(acc_ref)
        top_ref[...] = jnp.full_like(top_ref, TOP_START)
    for copy in kv_copies:
        copy.wait()
    count = jnp.int32(0)
    for i in range(n_buf * blk_dev):
        first_tag = blk_dev * block_len + (i % blk_dev) * tags
        tag = kv_buf[i // blk_dev, first_tag : first_tag + tags, :].astype(jnp.float32)
        request = jnp.max(tag[:, :HD]).astype(jnp.int32)
        offset = jnp.max(tag[:, HD:]).astype(jnp.int32) * block_len
        for tile in reversed(range(tiles)):
            item_ref[0, count] = i // blk_dev
            item_ref[4, count] = (i % blk_dev) * block_len
            item_ref[1, count] = request
            item_ref[2, count] = tile
            item_ref[3, count] = offset
            used = rows_smem[request, (tile + 1) * (rows // tiles) - 1] > offset
            count = count + jnp.where(used, 1, 0)
    for pad in range(2):
        item_ref[0, count + pad] = 0
        item_ref[4, count + pad] = 0
        item_ref[1, count + pad] = 0
        item_ref[2, count + pad] = 0
        item_ref[3, count + pad] = NOWHERE
    for copy in query_copies:
        copy.wait()
    scale = math.log2(math.e) / math.sqrt(HD)
    token = lax.broadcasted_iota(jnp.int32, (block_len, half), 0)

    def tokens_of(item):
        return pl.ds(pl.multiple_of(item_ref[4, item], 8), block_len)

    def score(item, score_ref, best_ref):
        i, request, tile = item_ref[0, item], item_ref[1, item], item_ref[2, item]
        scores = lax.dot_general(
            kv_buf[i, tokens_of(item), :HD],
            query_buf[request ^ mixed, tile],
            (((1,), (1,)), ((), ())),
            preferred_element_type=jnp.float32,
        )
        limit = wide_ref[tile * n_req + request] - item_ref[3, item]
        scores = jnp.where(token < limit, scores * scale, MASKED)
        score_ref[...] = scores
        best_ref[...] = jnp.max(scores, axis=0, keepdims=True)

    def add(item, score_ref, best_ref):
        i = item_ref[0, item]
        place = item_ref[2, item] * n_req + item_ref[1, item]
        old_top = top_ref[place]
        new_top = jnp.maximum(old_top, best_ref[...])
        factor = jnp.exp2(old_top - new_top)
        weights = jnp.exp2(score_ref[...] - new_top).astype(jnp.bfloat16)
        values = jnp.concatenate(
            [jnp.transpose(kv_buf[i, tokens_of(item), HD:]), jnp.ones((STATS, block_len), jnp.bfloat16)], axis=0
        )
        summed = jnp.dot(values, weights, preferred_element_type=jnp.float32)
        acc_ref[place] = acc_ref[place] * factor + summed[: HD + 8]
        top_ref[place] = new_top

    score(0, score_a, best_a)

    def two_items(j, carried):
        score(2 * j + 1, score_b, best_b)
        add(2 * j, score_a, best_a)
        score(2 * j + 2, score_a, best_a)
        add(2 * j + 1, score_b, best_b)
        return carried

    lax.fori_loop(0, (count + 1) // 2, two_items, 0)

    if last:
        for step, out_ref in enumerate(out_refs):
            request = step ^ mixed
            levels = []
            for tile in range(tiles):
                place = tile * n_req + request
                total = acc_ref[place, HD : HD + 1]
                some = total > 0.0
                safe = jnp.where(some, total, 1.0)
                result = acc_ref[place, :HD] * (1.0 / safe)
                out_ref[tile * half : (tile + 1) * half, :] = jnp.transpose(result).astype(jnp.bfloat16)
                level = jnp.where(some, top_ref[place] + jnp.log2(safe), TOP_START)
                levels += [level[:, at * HD : (at + 1) * HD] for at in range(half // HD)]
            level = jnp.concatenate(levels, axis=0)
            high = level.astype(jnp.bfloat16)
            rest = level - high.astype(jnp.float32)
            middle = rest.astype(jnp.bfloat16)
            low = (rest - middle.astype(jnp.float32)).astype(jnp.bfloat16)
            pieces = [high, middle, low, jnp.zeros((STATS - 3 * len(levels), HD), jnp.bfloat16)]
            out_ref[tiles * half :, :] = jnp.concatenate(pieces, axis=0)


def own_scores(n_sub, group_size, rows_ref, fresh_ref, *refs):
    query_refs, own_ref, wide_ref = refs[:-2], refs[-2], refs[-1]
    request = lax.axis_index("shard") // n_sub
    n_req, rows = rows_ref.shape
    kv_local = fresh_ref.shape[1] // (2 * HD)
    sub_heads = group_size // n_sub
    lines = sub_heads * rows // HD
    scale = math.log2(math.e) / math.sqrt(HD)
    own_ref[...] = jnp.zeros_like(own_ref)
    cosine, sine = row_turns(rows_ref[pl.ds(request, 1), :])
    for step, query_ref in enumerate(query_refs):
        kv_id = (step % kv_local) ^ (request % kv_local)
        column = pl.multiple_of(2 * kv_id * HD, HD)
        own_key = turn(fresh_ref[:, pl.ds(column, HD)], cosine, sine).astype(jnp.float32)
        for head, row_part, flat in chunks_of(sub_heads, rows):
            query = query_ref[flat, :].astype(jnp.float32)
            line, at = step * lines + flat.start // HD, flat.start % HD
            own = jnp.sum(query * own_key[row_part, :], axis=1, keepdims=True) * scale
            own_ref[at : at + own.shape[0], line : line + 1] = own
    tiles = tiles_of(sub_heads * rows)
    size = rows // tiles
    for tile in range(tiles):
        wide = jnp.concatenate([rows_ref[:, tile * size : (tile + 1) * size]] * sub_heads, axis=1)
        for r in range(n_req):
            wide_ref[tile * n_req + r] = wide[r : r + 1]


def merge_own(n_sub, group_size, own_ref, fresh_ref, *refs):
    part_refs, (out_ref, level_ref, out_buf, out_sem) = refs[:-4], refs[-4:]
    request = lax.axis_index("shard") // n_sub
    rows = out_ref.shape[0]
    copies = []
    kv_local = fresh_ref.shape[1] // (2 * HD)
    sub_heads = group_size // n_sub
    width = sub_heads * rows
    lines = width // HD
    level_ref[...] = jnp.zeros_like(level_ref)
    for step, part_ref in enumerate(part_refs):
        stats = part_ref[width:, :].astype(jnp.float32)
        level_ref[step * lines : (step + 1) * lines] = stats[:lines] + stats[lines : 2 * lines] + stats[2 * lines : 3 * lines]
    level = jnp.transpose(level_ref[...])
    own = own_ref[...]
    top = jnp.maximum(own, level)
    own_share = jnp.exp2(own - top)
    share = jnp.exp2(level - top)
    norm = 1.0 / (own_share + share)
    own_share, share = own_share * norm, share * norm
    for step, part_ref in enumerate(part_refs):
        kv_id = (step % kv_local) ^ (request % kv_local)
        sub = (step // kv_local) ^ (request // kv_local)
        value_column = pl.multiple_of((2 * kv_id + 1) * HD, HD)
        own_value = fresh_ref[:, pl.ds(value_column, HD)].astype(jnp.float32)
        for head, row_part, flat in chunks_of(sub_heads, rows):
            line, at = step * lines + flat.start // HD, flat.start % HD
            size = flat.stop - flat.start
            part = part_ref[flat, :].astype(jnp.float32)
            out_buf[step, row_part, head * HD : (head + 1) * HD] = (
                part * share[at : at + size, line : line + 1]
                + own_value[row_part, :] * own_share[at : at + size, line : line + 1]
            ).astype(jnp.bfloat16)
        span = sub_heads * HD
        column = pl.multiple_of((kv_id * group_size + sub * sub_heads) * HD, HD)
        copies.append(pltpu.make_async_copy(out_buf.at[step], out_ref.at[:, pl.ds(column, span)], out_sem.at[step]))
        copies[-1].start()
    for copy in copies:
        copy.wait()


def moved(x, pairs):
    return lax.ppermute(x, "shard", pairs)


def shards(kv_store, block_order, lengths, row_positions, queries, fresh_rows):
    n_shard = lax.axis_size("shard")
    n_req, rows = row_positions.shape
    n_sub = n_shard // n_req
    blk_dev, block_len, full_width = kv_store.shape
    kv_heads = full_width // (2 * HD)
    kv_local = kv_heads // n_sub
    group_size = queries.shape[1] // (kv_local * HD)
    sub_heads = group_size // n_sub
    width = sub_heads * rows
    tiles = tiles_of(width)
    half_width = width // tiles
    bf16 = jnp.bfloat16
    spec = functools.partial(pl.BlockSpec, memory_space=VMEM)
    smem = pl.BlockSpec(memory_space=SMEM)
    anywhere = pl.BlockSpec(memory_space=pl.ANY)

    grant = pltpu.CompilerParams(vmem_limit_bytes=GRANT)
    sent_queries = pl.pallas_call(
        functools.partial(pack_queries, n_sub, group_size),
        out_shape=[jax.ShapeDtypeStruct((width, HD), bf16)] * n_req,
        in_specs=[anywhere] * 2,
        out_specs=[spec()] * n_req,
        scratch_shapes=[
            pltpu.VMEM((rows, HD), jnp.float32),
            pltpu.VMEM((rows, HD), jnp.float32),
            pltpu.VMEM((n_req, rows), jnp.int32),
            pltpu.VMEM((kv_local, rows, group_size * HD), bf16),
            pltpu.SemaphoreType.DMA((kv_local + 1,)),
        ],
        compiler_params=grant,
        name="pack_queries",
    )(row_positions, queries)
    level_rows = max(HD, n_req * width // HD)
    own, wide_rows = pl.pallas_call(
        functools.partial(own_scores, n_sub, group_size),
        out_shape=[
            jax.ShapeDtypeStruct((rows, level_rows), jnp.float32),
            jax.ShapeDtypeStruct((n_req * tiles, 1, width // tiles), jnp.int32),
        ],
        in_specs=[spec()] * (2 + n_req),
        out_specs=[spec()] * 2,
        compiler_params=grant,
        name="own_scores",
    )(row_positions, fresh_rows, *sent_queries)
    lengths_after = lax.optimization_barrier((lengths, sent_queries[0]))[0]

    packed_kv = pl.pallas_call(
        functools.partial(pack_kv, n_sub),
        out_shape=[jax.ShapeDtypeStruct((blk_dev * block_len + TAG, 2 * HD), bf16)] * kv_heads,
        in_specs=[smem, smem, anywhere],
        out_specs=[spec()] * kv_heads,
        scratch_shapes=[pltpu.VMEM((blk_dev, block_len, full_width), bf16), pltpu.SemaphoreType.DMA((blk_dev,))],
        compiler_params=grant,
        name="pack_kv",
    )(block_order, lengths_after, kv_store)

    to_compute = []
    for step in range(n_req):
        pairs = []
        for request in range(n_req):
            for h in range(n_sub):
                head = kv_local * h + ((step % kv_local) ^ (request % kv_local))
                sub = (step // kv_local) ^ (request // kv_local)
                pairs.append((request * n_sub + h, head * n_sub + sub))
        to_compute.append(pairs)
    held_queries = [moved(x, pairs) for x, pairs in zip(sent_queries, to_compute)]


    def after(x, *others):
        return lax.optimization_barrier((x, *others))[0] if others else x

    def at_head(mask, *others):
        pairs = [(d, ((d // n_sub) ^ mask) * n_sub + d % n_sub) for d in range(n_shard)]
        return packed_kv[0] if mask == 0 else moved(after(packed_kv[mask], *others), pairs)

    def from_sub(mask, back, *others):
        x = landed[mask]
        pairs = [(d, (d // n_sub) * n_sub + (d % n_sub + back) % n_sub) for d in range(n_shard)]
        return x if back == 0 else moved(after(x, *others), pairs)

    half = kv_heads // 2
    groups = [[0], list(range(1, half)), [half, half + 1]] + [[mask] for mask in range(half + 2, kv_heads)]
    landed = {mask: at_head(mask) for mask in range(half + 2)}
    landed[half + 2] = at_head(half + 2, *held_queries)
    state_shapes = [
        pltpu.VMEM((n_req * tiles, HD + 8, half_width), jnp.float32),
        pltpu.VMEM((n_req * tiles, 1, half_width), jnp.float32),
        pltpu.VMEM((n_req, tiles, half_width, HD), bf16),
    ]
    part_shapes = [jax.ShapeDtypeStruct((width + STATS, HD), bf16)] * n_req
    parts = [[(mask, back) for mask in masks for back in range(n_sub)] for masks in groups]
    parts[-1:] = [parts[-1][:1], parts[-1][1:]]
    state, gate = [], []
    for index, buffers in enumerate(parts):
        if index == 1:
            for mask in range(half + 3, kv_heads):
                if mask not in landed:
                    landed[mask] = at_head(mask, landed[half])
        first, last = index == 0, index == len(parts) - 1
        gate = gate if last else state[-1:]
        arrived = [from_sub(mask, back, *gate) for mask, back in buffers]
        blocks = len(buffers) * blk_dev
        inputs = [*(held_queries if first else []), *arrived]
        results = pl.pallas_call(
            functools.partial(attend, n_sub, len(buffers), first, last, blk_dev),
            out_shape=(part_shapes if last else []) + state_shapes,
            in_specs=[smem, spec()] + [anywhere] * len(inputs) + [spec()] * len(state),
            out_specs=[spec()] * ((n_req if last else 0) + 3),
            input_output_aliases={2 + len(inputs) + k: (n_req if last else 0) + k for k in range(len(state))},
            scratch_shapes=[
                pltpu.VMEM((len(buffers), blk_dev * block_len + TAG, 2 * HD), bf16),
                pltpu.VMEM((block_len, half_width), jnp.float32),
                pltpu.VMEM((block_len, half_width), jnp.float32),
                pltpu.VMEM((1, half_width), jnp.float32),
                pltpu.VMEM((1, half_width), jnp.float32),
                pltpu.SMEM((5, blocks * tiles + 2), jnp.int32),
                pltpu.SemaphoreType.DMA((n_req, tiles)),
                pltpu.SemaphoreType.DMA((len(buffers),)),
            ],
            compiler_params=grant,
        )(row_positions, wide_rows, *inputs, *state)
        state = list(results)
    returned = [moved(part, [(b, a) for a, b in pairs]) for part, pairs in zip(state, to_compute)]

    return pl.pallas_call(
        functools.partial(merge_own, n_sub, group_size),
        out_shape=jax.ShapeDtypeStruct((rows, kv_local * group_size * HD), bf16),
        in_specs=[spec()] * (2 + n_req),
        out_specs=anywhere,
        scratch_shapes=[
            pltpu.VMEM((level_rows, rows), jnp.float32),
            pltpu.VMEM((n_req, rows, sub_heads * HD), bf16),
            pltpu.SemaphoreType.DMA((n_req,)),
        ],
        compiler_params=grant,
        name="merge_own",
    )(own, fresh_rows, *returned)


def solution(mesh):
    in_specs = (
        P(("groups", "shard"), None, None),
        P(("groups", "shard")),
        P("groups"),
        P("groups", None),
        P("groups", "shard"),
        P("groups", "shard"),
    )
    return jax.shard_map(shards, mesh=mesh, in_specs=in_specs, out_specs=P("groups", "shard"), check_vma=False)
```
